256 devices in a mesh: section: 4 (over x), seq: 32 (over z, y), mp: 2 (over core).
Axes of the slice: x: 4, y: 4, z: 8, core: 2. Of those that a mesh axis runs over, the one named last changes fastest.
Arguments:
- text_embed: bfloat16 [320, 8192], P(None, ('seq', 'mp')), may hold values from -6 to 6
- patch_hidden: bfloat16 [256, 5120], P(('section', 'seq', 'mp')), may hold values from -8 to 8
- merge_weight: bfloat16 [5120, 8192], P(None, ('seq', 'mp')), may hold values from -0.078125 to 0.078125
- merge_bias: bfloat16 [8192], P(('seq', 'mp')), may hold values from -3 to 3
- norm_gain: bfloat16 [4, 8192], P('section'), may hold values from 0.5 to 1.5
- query_weight: bfloat16 [4, 8192, 8192], P('section', None, ('seq', 'mp')), may hold values from -0.62285876 to 0.62285876
- key_weight: bfloat16 [4, 8192, 1024], P('section', None, ('seq', 'mp')), may hold values from -0.62285876 to 0.62285876
- value_weight: bfloat16 [4, 8192, 1024], P('section', None, ('seq', 'mp')), may hold values from -0.055242717 to 0.055242717
- image_counts: int32 [2, 4], replicated, may hold values from 1 to 64, 128 in all within a row
- text_counts: int32 [2, 4], replicated, may hold values from 1 to 16, 32 in all within a row
Outputs:
- hidden_states: bfloat16 [4, 320, 8192], P('section', None, ('seq', 'mp'))
The draws below stay inside these ranges and needn't reach their ends.
Inputs may be any that keep to these rules, and one draw needn't show every extreme that they name: `image_counts`: each micro-batch's image counts sum to 256 / 2. `text_counts`: each micro-batch's image and text counts together sum to 160.
All inputs are finite; a program needn't handle non-finite values.
Results may differ from the reference program's by a relative error of at most 0.017.
Values may be sent and summed in bfloat16 or wider, within the bound.
A program may use at most 64 MiB of HBM per device.

```python
import math
import jax
import jax.numpy as jnp
import numpy as np
from jax import lax

D = 8192
HEADS = 64
HD = 128
KV_HEADS = 8
VIN = 5120
LAYERS = 4
MB = 2
REQ = 4
NT = 160
IMG_ROWS = 256
TOKENS = 320


def draw_text_embed(key, part):
    values = jnp.clip(jax.random.normal(jax.random.fold_in(key, 101), (TOKENS, D), jnp.float32), -6.0, 6.0)
    return values.astype(jnp.bfloat16)


def draw_query_weight(key, part):
    values = jnp.clip(jax.random.normal(jax.random.fold_in(key, 102), (LAYERS, D, D), jnp.float32), -5.0, 5.0) / math.sqrt(D)
    return values.astype(jnp.bfloat16)


def draw_key_weight(key, part):
    values = jnp.clip(jax.random.normal(jax.random.fold_in(key, 103), (LAYERS, D, KV_HEADS * HD), jnp.float32), -5.0, 5.0) / math.sqrt(D)
    return values.astype(jnp.bfloat16)


def draw_value_weight(key, part):
    values = jnp.clip(jax.random.normal(jax.random.fold_in(key, 104), (LAYERS, D, KV_HEADS * HD), jnp.float32), -5.0, 5.0) / math.sqrt(D)
    return values.astype(jnp.bfloat16)


def block_levels(key, dims, cuts, smallest, largest):
    gain, own = 1.0, jax.random.fold_in(key, 6)
    for dim, blocks in cuts:
        draws = jnp.exp(jax.random.uniform(jax.random.fold_in(own, dim), (blocks,), jnp.float32, smallest / len(cuts), largest / len(cuts)))
        gain = gain * jnp.repeat(draws, dims[dim] // blocks).reshape([-1 if axis == dim else 1 for axis in range(len(dims))])
    return gain


def length_profile(amount, total, reach, skew):
    loads = [(1 << 20) // math.isqrt(standing ** skew) + 1 for standing in range(2, amount + 1)]
    surplus, given = total - reach - (amount - 1), [1] * (amount - 1)
    while surplus > 0:
        free = [i for i in range(amount - 1) if given[i] < reach]
        mass, left = sum([loads[i] for i in free]), surplus
        for i in free:
            extra = min(reach - given[i], max(1, left * loads[i] // mass), surplus)
            given[i] = given[i] + extra
            surplus = surplus - extra
    return np.array([reach] + given)


def ragged(key, amount, total, limit, skew):
    if amount == 2:
        one = jax.random.randint(key, (), max(1, total - limit), min(limit, total - 1) + 1)
        return jnp.stack([one, total - one])
    sizes = jnp.asarray(length_profile(amount, total, limit, skew), jnp.int32)
    couples = (amount - 1) // 2
    donor, receiver = sizes[1:1 + 2 * couples:2], sizes[2:2 + 2 * couples:2]
    margin = jnp.minimum(donor - 1, limit - receiver)
    moved = jax.random.randint(jax.random.fold_in(key, 1), (couples,), 0, 1 << 20) % (margin + 1)
    sizes = sizes.at[1:1 + 2 * couples:2].set(donor - moved).at[2:2 + 2 * couples:2].set(receiver + moved)
    return sizes[jax.random.permutation(jax.random.fold_in(key, 2), amount)]


def gaussian(own_key, extent, deviation, reach, split=(), held_as=jnp.bfloat16):
    gain = block_levels(own_key, extent, split, -0.22, 0.18) if split else 1.0
    result = jax.random.normal(own_key, extent, jnp.float32) * deviation * gain
    return jnp.minimum(jnp.maximum(result, -reach), reach).astype(held_as)


def setup_inputs(seed: int = 0) -> dict:
    arg_keys = jax.random.split(jax.random.key(seed), 11)
    text_embed = draw_text_embed(jax.random.fold_in(arg_keys[10], 71), 0)
    patch_hidden = gaussian(arg_keys[1], (IMG_ROWS, VIN), 1.5, 8.0, ((0, 256),))
    merge_weight = gaussian(arg_keys[2], (VIN, D), VIN ** -0.5, 0.078125, ((1, 64),))
    merge_bias = gaussian(arg_keys[3], (D,), 0.5, 3.0, ((0, 64),))
    norm_gain = jnp.clip(1.0 + 0.1 * jax.random.normal(arg_keys[4], (LAYERS, D), jnp.float32), 0.5, 1.5).astype(jnp.bfloat16)
    query_weight = draw_query_weight(jax.random.fold_in(arg_keys[10], 71), 0)
    key_weight = draw_key_weight(jax.random.fold_in(arg_keys[10], 71), 0)
    value_weight = draw_value_weight(jax.random.fold_in(arg_keys[10], 71), 0)
    image_counts = jax.vmap(lambda own: ragged(own, REQ, IMG_ROWS // MB, IMG_ROWS // MB // 2, 2))(jax.random.split(arg_keys[8], MB)).reshape((MB, REQ)).astype(jnp.int32)
    text_counts = jax.vmap(lambda own: ragged(own, REQ, NT - IMG_ROWS // MB, (NT - IMG_ROWS // MB) // 2, 1))(jax.random.split(arg_keys[9], MB)).reshape((MB, REQ)).astype(jnp.int32)
    return {"text_embed": text_embed, "patch_hidden": patch_hidden, "merge_weight": merge_weight, "merge_bias": merge_bias, "norm_gain": norm_gain, "query_weight": query_weight, "key_weight": key_weight, "value_weight": value_weight, "image_counts": image_counts, "text_counts": text_counts}


def layout(image_counts, text_counts, tokens):
    lengths = (image_counts + text_counts).reshape(-1).astype(jnp.int32)
    images = image_counts.reshape(-1).astype(jnp.int32)
    ends = jnp.cumsum(lengths).astype(jnp.int32)
    starts = (ends - lengths).astype(jnp.int32)
    before = (jnp.cumsum(images) - images).astype(jnp.int32)
    position = jnp.arange(tokens, dtype=jnp.int32)
    request = lax.optimization_barrier(jnp.sum((position[:, None] >= ends[None, :]).astype(jnp.int32), axis=1)).astype(jnp.int32)
    member = request[:, None] == jnp.arange(lengths.shape[0], dtype=jnp.int32)[None, :]
    first = lax.optimization_barrier(jnp.sum(jnp.where(member, starts[None, :], 0), axis=1)).astype(jnp.int32)
    count = lax.optimization_barrier(jnp.sum(jnp.where(member, images[None, :], 0), axis=1)).astype(jnp.int32)
    earlier = lax.optimization_barrier(jnp.sum(jnp.where(member, before[None, :], 0), axis=1)).astype(jnp.int32)
    offset = (position - first).astype(jnp.int32)
    is_image = (offset >= 1) & (offset <= count)
    row_index = jnp.where(is_image, earlier + offset - 1, 0).astype(jnp.int32)
    return (request, is_image, row_index)

def reference(text_embed, patch_hidden, merge_weight, merge_bias, norm_gain, query_weight, key_weight, value_weight, image_counts, text_counts):
    act = jax.nn.gelu(patch_hidden.astype(jnp.float32), approximate=False).astype(jnp.bfloat16)
    merged = (jnp.dot(act, merge_weight, preferred_element_type=jnp.float32) + merge_bias.astype(jnp.float32)).astype(jnp.bfloat16)
    tokens = text_embed.shape[0]
    group_size = HEADS // KV_HEADS
    request, is_image, row_index = layout(image_counts, text_counts, tokens)
    state = jnp.where(is_image[:, None], merged[row_index], text_embed)
    position = jnp.arange(tokens, dtype=jnp.int32)
    allowed = (request[:, None] == request[None, :]) & (position[None, :] <= position[:, None])
    outputs = []
    for layer in range(LAYERS):
        xf = state.astype(jnp.float32)
        scale = lax.rsqrt(lax.optimization_barrier(jnp.mean(xf * xf, axis=1, keepdims=True)) + 1e-06)
        normed = (xf * scale * norm_gain[layer].astype(jnp.float32)[None, :]).astype(jnp.bfloat16)
        query = jnp.dot(normed, query_weight[layer], preferred_element_type=jnp.float32).astype(jnp.bfloat16).reshape(tokens, KV_HEADS, group_size, HD)
        key = jnp.dot(normed, key_weight[layer], preferred_element_type=jnp.float32).astype(jnp.bfloat16).reshape(tokens, HD, KV_HEADS).transpose(0, 2, 1)
        value = jnp.dot(normed, value_weight[layer], preferred_element_type=jnp.float32).astype(jnp.bfloat16).reshape(tokens, HD, KV_HEADS).transpose(0, 2, 1)
        scores = jnp.einsum('qngd,knd->ngqk', query.astype(jnp.float32), key.astype(jnp.float32)) / math.sqrt(HD)
        scores = jnp.where(allowed[None, None, :, :], scores, -1e+30)
        probs = jax.nn.softmax(scores, axis=-1).astype(jnp.bfloat16)
        attended = jnp.einsum('ngqk,knd->qngd', probs.astype(jnp.float32), value.astype(jnp.float32)).reshape(tokens, HEADS * HD)
        state = (xf + attended).astype(jnp.bfloat16)
        outputs.append(state)
    return jnp.stack(outputs)
```

```python
import functools
import math

import jax
import jax.numpy as jnp
from jax import lax
from jax.experimental import pallas as pl
from jax.experimental.pallas import tpu as pltpu
from jax.sharding import PartitionSpec as P

MESH = pl.DeviceIdType.MESH
F32 = jnp.float32
BF16 = jnp.bfloat16
HD = 128
NY = 4
NZ = 8
CHUNKS = 4
Z_ORDER = (4, 3, 5, 2, 6, 1, 7)


def iota(shape, dim):
    return lax.broadcasted_iota(jnp.int32, shape, dim)


def dot(a, b):
    return lax.dot_general(a, b, (((1,), (0,)), ((), ())), preferred_element_type=F32)


def dot_t(a, b):
    return lax.dot_general(a, b, (((1,), (1,)), ((), ())), preferred_element_type=F32)


def drain(ref, sem):
    pltpu.make_async_copy(ref, ref, sem).wait()


def kernel(
    images_ref,
    texts_ref,
    text_ref,
    patch_ref,
    mw_ref,
    bias_ref,
    gain_ref,
    wq_ref,
    wk_ref,
    wv_ref,
    out_ref,
    gains,
    actf,
    act,
    rows,
    rowsf,
    part,
    merged,
    start,
    kvtx,
    kvrx,
    kvrows,
    kvmine,
    wq_sib,
    weights,
    states,
    xs,
    xr,
    kvx,
    spread,
    keys,
    values,
    s_act,
    r_act1,
    r_act2,
    r_act3,
    s_wq,
    r_wq,
    s_kv,
    r_kv,
    s_kvm,
    r_kvm,
    s_part,
    r_part,
    s_init,
    s_st,
    r_st,
    s_fw,
    r_fw,
    s_x,
    r_x,
    s_kx,
    r_kx,
):
    sec = lax.axis_index("section")
    seq = lax.axis_index("seq")
    core = lax.axis_index("mp")
    depth = lax.axis_size("section")
    z = seq // NY
    y = seq % NY
    tokens = out_ref.shape[0]
    tc = tokens // CHUNKS
    batch = tokens // images_ref.shape[0]
    per_batch = batch // tc

    def at_z(dz, s=None):
        return (sec if s is None else s, ((z + dz) % NZ) * NY + y, core)

    def at_y(dy):
        return (sec, z * NY + (y + dy) % NY, core)

    sibling = (sec, seq, 1 - core)

    def send(src, dst, ssem, rsem, device):
        pltpu.make_async_remote_copy(
            src_ref=src, dst_ref=dst, send_sem=ssem, recv_sem=rsem, device_id=device, device_id_type=MESH
        ).start()

    barrier = pltpu.get_barrier_semaphore()

    def greet(device):
        pl.semaphore_signal(barrier, inc=1, device_id=device, device_id_type=MESH)

    for dz in Z_ORDER:
        greet(at_z(dz))
    for dy in (2, 1, 3):
        greet(at_y(dy))
    greet(sibling)

    @pl.when(sec > 0)
    def _():
        for dz in (0,) + Z_ORDER:
            greet(at_z(dz, sec - 1))

    @pl.when(sec == 0)
    def _():
        for other in (1, 2, 3):
            greet((other, seq, core))

    for k in range(40):
        actf[k : k + 1, :] = patch_ref[:, k * 128 : (k + 1) * 128].astype(F32)
    xa = actf[...]
    act[...] = (0.5 * xa * (1.0 + lax.erf(xa * math.sqrt(0.5)))).astype(BF16)
    for k in range(64):
        gains[k : k + 1, :] = gain_ref[:, k * 128 : (k + 1) * 128].astype(F32)

    r_i, c_i = iota((128, 128), 0), iota((128, 128), 1)
    deal = (
        ((r_i >> 4) == (c_i & 7)) & (((r_i >> 2) & 3) == (c_i >> 5)) & ((r_i & 3) == ((c_i >> 3) & 3))
    )
    deal = jnp.where(deal, 1.0, 0.0).astype(BF16)
    for t in range(16):
        pieces = []
        for b in range(4):
            lanes = slice((4 * t + b) * 128, (4 * t + b + 1) * 128)
            pieces += [wk_ref[:, lanes], wv_ref[:, lanes]]
        kvtx[:, t] = dot(deal, jnp.concatenate(pieces, axis=0)).astype(BF16).reshape(NZ, 16, 128)
    for q in range(32):
        kvmine[q // NY, q % NY, 2] = jnp.zeros((32, 128), BF16)
        kvmine[q // NY, q % NY, 3] = jnp.zeros((32, 128), BF16)
    r_i, c_i = iota((512, 256), 0), iota((512, 256), 1)
    lane = r_i & 127
    feature = 2 * ((lane & 7) * 8 + (r_i >> 7) * 2 + ((lane >> 5) & 1)) + ((lane >> 3) & 1)
    natural = (lane < 64) & (c_i == ((lane >> 4) & 1) * 128 + feature)
    spread[...] = jnp.where(natural, 1.0, 0.0).astype(BF16)

    @pl.when(sec == 0)
    def _():
        pl.semaphore_wait(barrier, 19)

    @pl.when((sec > 0) & (sec < depth - 1))
    def _():
        pl.semaphore_wait(barrier, 20)

    @pl.when(sec == depth - 1)
    def _():
        pl.semaphore_wait(barrier, 12)

    for dz in Z_ORDER:
        send(act, rows.at[core, z, y], s_act.at[0], r_act1, at_z(dz))
    pltpu.make_async_copy(act, rows.at[core, z, y], r_act1).start()
    send(wq_ref.at[:, :, 1 - core], wq_sib, s_wq, r_wq, sibling)

    def scaled(q, w):
        g = gains[pl.ds(2 * q + core, 1), :]
        d = jnp.where(iota((128, 128), 0) == iota((128, 128), 1), g, 0.0).astype(BF16)
        return d, dot(d, w).astype(BF16)

    @pl.loop(0, 32)
    def _(q):
        zz, yy = q // NY, q % NY
        weights[zz, yy, :, 0:128] = scaled(q, wq_ref[zz, yy, core])[1]

    drain(rows.at[core, :, 0], r_act1)
    for i, dy in enumerate((2, 1, 3)):
        send(rows.at[core, :, y], rows.at[core, :, y], s_act.at[1], r_act2, at_y(dy))
    for dz in Z_ORDER:
        send(kvtx.at[(z + dz) % NZ], kvrx.at[z], s_kv, r_kv, at_z(dz))
    pltpu.make_async_copy(kvtx.at[z], kvrx.at[z], r_kv).start()

    drain(wq_sib, r_wq)

    @pl.loop(0, 32)
    def _(q):
        zz, yy = q // NY, q % NY
        weights[zz, yy, :, 128:256] = scaled(q, wq_sib[zz, yy])[1]

    drain(rows.at[core, :, pl.ds(0, 3)], r_act2)
    send(rows.at[core], rows.at[core], s_act.at[2], r_act3, sibling)
    drain(rows.at[core], r_act3)

    for p in range(2):
        for zz in range(NZ):
            for yy in range(NY):
                at = ((p * NZ + zz) * NY + yy) * 40
                rowsf[at : at + 40, :] = rows[p, zz, yy].astype(F32)
    acc = jnp.broadcast_to(bias_ref[...].astype(F32), (64, 128))
    for k in range(20):
        xk = jnp.concatenate(
            [rowsf[pl.ds(2 * k, 64, stride=40), :], rowsf[pl.ds(2 * k + 1, 64, stride=40), :]], axis=1
        ).astype(BF16)
        acc = acc + dot(xk, mw_ref[256 * k : 256 * (k + 1), :])
    part[...] = acc.astype(BF16)

    @pl.when(sec > 0)
    def _():
        send(part, merged.at[sec], s_part, r_part, (0, seq, core))

    def place(rows_here, first):
        pos = first + iota((rows_here, 1), 0)
        begin = jnp.zeros((rows_here, 1), jnp.int32)
        count = jnp.zeros((rows_here, 1), jnp.int32)
        earlier = jnp.zeros((rows_here, 1), jnp.int32)
        at, seen = jnp.int32(0), jnp.int32(0)
        for b in range(images_ref.shape[0]):
            for r in range(images_ref.shape[1]):
                image, text = images_ref[b, r], texts_ref[b, r]
                inside = pos >= at
                begin = jnp.where(inside, at, begin)
                count = jnp.where(inside, image, count)
                earlier = jnp.where(inside, seen, earlier)
                at, seen = at + image + text, seen + image
        return pos, begin, count, earlier

    @pl.when(sec == 0)
    def _():
        merged[0] = part[...]
        pos, begin, count, earlier = place(tokens, 0)
        offset = pos - begin
        is_image = (offset >= 1) & (offset <= count)
        row = earlier + offset - 1
        slot = (row & ~63) + ((row & 1) << 5) + ((row & 63) >> 1)
        chosen = (iota((tokens, 256), 1) == slot) & is_image
        drain(merged.at[pl.ds(1, 3)], r_part)
        picked = dot(jnp.where(chosen, 1.0, 0.0).astype(BF16), merged[...].reshape(256, 128))
        start[...] = jnp.where(is_image, picked, text_ref[...].astype(F32)).astype(BF16)
        for t in range(CHUNKS):
            src = start.at[pl.ds(t * tc, tc)]
            for dz in Z_ORDER:
                send(src, states.at[t, z, y], s_init.at[t], r_st.at[t], at_z(dz))
            pltpu.make_async_copy(src, states.at[t, z, y], r_st.at[t]).start()

    drain(kvrx, r_kv)
    r_i, c_i = iota((128, 128), 0), iota((128, 128), 1)
    collect = ((r_i >> 5) == ((c_i >> 2) & 3)) & (((r_i >> 3) & 3) == (c_i & 3)) & ((r_i & 7) == (c_i >> 4))
    collect = jnp.where(collect, 1.0, 0.0).astype(BF16)
    for t in range(16):
        made = dot(collect, kvrx[:, t].reshape(128, 128)).astype(BF16).reshape(2, 2, 32, 128)
        for h in range(2):
            kvrows[t // 2, (t % 2) * 2 + h] = made[h]
    send(kvrows.at[:, :, 1 - core], kvmine.at[:, :, core], s_kvm, r_kvm, sibling)
    mine = pltpu.make_async_copy(kvrows.at[:, :, core], kvmine.at[:, :, core], s_kvm)
    mine.start()

    def forward(t):
        drain(states.at[t, :, 0], r_st.at[t])
        for dy in (2, 1, 3):
            send(states.at[t, :, y], states.at[t, :, y], s_fw.at[t], r_fw.at[t], at_y(dy))

    forward(0)
    drain(kvmine.at[:, :, 0], r_kvm)
    drain(kvmine.at[:, :, pl.ds(0, 2)], s_kvm)

    @pl.loop(0, 32)
    def _(q):
        zz, yy = q // NY, q % NY
        g = gains[pl.ds(2 * q + core, 1), :]
        d = jnp.where(iota((128, 128), 0) == iota((128, 128), 1), g, 0.0).astype(BF16)
        weights[zz, yy, :, 256:384] = dot_t(d, kvmine[zz, yy].reshape(128, 128)).astype(BF16)

    for t in range(CHUNKS):
        if t + 1 < CHUNKS:
            forward(t + 1)
        drain(states.at[t, :, pl.ds(0, 3)], r_fw.at[t])

        def products(zz, carry):
            acc, squares = carry
            x = jnp.concatenate([states[t, zz, yy] for yy in range(NY)], axis=1)
            acc = acc + dot(x, weights[zz].reshape(NY * 128, 384))
            xf = x.astype(F32)
            for yy in range(NY):
                piece = xf[:, yy * 128 : (yy + 1) * 128]
                squares = squares + piece * piece
            return acc, squares

        acc, squares = lax.fori_loop(
            0, NZ, products, (jnp.zeros((tc, 384), F32), jnp.zeros((tc, 128), F32)), unroll=2
        )
        total = jnp.sum(squares, axis=1, keepdims=True)
        low = iota((tc, 128), 1) < 64
        mixed = jnp.where(low, acc[:, 256:384], total)
        xs[t, :, 0:128] = acc[:, 128:256]
        xs[t, :, 128:256] = mixed
        send(xs.at[t], xr.at[t], s_x.at[t], r_x.at[t], sibling)
        own = acc[:, 0:128]
        pos, begin, _, _ = place(tc, t * tc)
        drain(xr.at[t], r_x.at[t])
        mixed = mixed + xr[t, :, 128:256]
        scale = lax.rsqrt(mixed[:, 64:65] * (1.0 / 8192.0) + 1e-6)
        kvx[t, y] = jnp.where(low, mixed * scale, 0.0).astype(BF16)
        for dy in (2, 1, 3):
            send(kvx.at[t, y], kvx.at[t, y], s_kx.at[t], r_kx.at[t], at_y(dy))
        query = ((own + xr[t, :, 0:128]) * scale).astype(BF16)
        first = (t // per_batch) * batch
        span = (t % per_batch + 1) * tc
        column = first + iota((tc, span), 1)
        allowed = (column >= begin) & (column <= pos)
        drain(kvx.at[t, pl.ds(0, 3)], r_kx.at[t])
        kv = dot(jnp.concatenate([kvx[t, yy] for yy in range(NY)], axis=1), spread[...]).astype(BF16)
        keys[t * tc : (t + 1) * tc, :] = kv[:, 0:128]
        values[t * tc : (t + 1) * tc, :] = kv[:, 128:256]
        scores = dot_t(query, keys[first : first + span, :]) * (1.0 / math.sqrt(HD))
        scores = jnp.where(allowed, scores, -1e30)
        weight = jnp.exp(scores - jnp.max(scores, axis=1, keepdims=True))
        probs = (weight / jnp.sum(weight, axis=1, keepdims=True)).astype(BF16)
        attended = dot(probs, values[first : first + span, :])
        state = states[t, z, y].astype(F32) + attended
        out_ref[t * tc : (t + 1) * tc, :] = state.astype(BF16)

        @pl.when(sec < depth - 1)
        def _():
            for dz in Z_ORDER + (0,):
                send(
                    out_ref.at[pl.ds(t * tc, tc)], states.at[t, z, y], s_st.at[t], r_st.at[t], at_z(dz, sec + 1)
                )

    drain(rows.at[core, pl.ds(0, 7), 0], s_act.at[0])
    drain(rows.at[core, :, pl.ds(0, 3)], s_act.at[1])
    drain(rows.at[core], s_act.at[2])
    drain(wq_sib, s_wq)
    drain(kvrx.at[pl.ds(0, 7)], s_kv)

    @pl.when(sec > 0)
    def _():
        drain(part, s_part)

    for t in range(CHUNKS):

        @pl.when(sec == 0)
        def _():
            drain(states.at[t, pl.ds(0, 7), 0], s_init.at[t])

        @pl.when(sec < depth - 1)
        def _():
            drain(states.at[t, :, 0], s_st.at[t])

        drain(states.at[t, :, pl.ds(0, 3)], s_fw.at[t])
        drain(xs.at[t], s_x.at[t])
        drain(kvx.at[t, pl.ds(0, 3)], s_kx.at[t])


def shards(text_embed, patch, mw, bias, gain, wq, wk, wv, images, texts):
    tokens = text_embed.shape[0]
    tc = tokens // CHUNKS
    vmem = pl.BlockSpec(memory_space=pltpu.VMEM)
    smem = pl.BlockSpec(memory_space=pltpu.SMEM)
    dma = pltpu.SemaphoreType.DMA
    scratch = [
        pltpu.VMEM((64, 128), F32),
        pltpu.VMEM((40, 128), F32),
        pltpu.VMEM((40, 128), BF16),
        pltpu.VMEM((2, NZ, NY, 40, 128), BF16),
        pltpu.VMEM((2560, 128), F32),
        pltpu.VMEM((64, 128), BF16),
        pltpu.VMEM((4, 64, 128), BF16),
        pltpu.VMEM((tokens, 128), BF16),
        pltpu.VMEM((NZ, 16, 16, 128), BF16),
        pltpu.VMEM((NZ, 16, 16, 128), BF16),
        pltpu.VMEM((NZ, NY, 2, 32, 128), BF16),
        pltpu.VMEM((NZ, NY, 4, 32, 128), BF16),
        pltpu.VMEM((NZ, NY, 128, 128), BF16),
        pltpu.VMEM((NZ, NY, 128, 384), BF16),
        pltpu.VMEM((CHUNKS, NZ, NY, tc, 128), BF16),
        pltpu.VMEM((CHUNKS, tc, 256), F32),
        pltpu.VMEM((CHUNKS, tc, 256), F32),
        pltpu.VMEM((CHUNKS, NY, tc, 128), BF16),
        pltpu.VMEM((512, 256), BF16),
        pltpu.VMEM((tokens, 128), BF16),
        pltpu.VMEM((tokens, 128), BF16),
        dma((3,)),
        dma,
        dma,
        dma,
        dma,
        dma,
        dma,
        dma,
        dma,
        dma,
        dma,
        dma,
        dma((CHUNKS,)),
        dma((CHUNKS,)),
        dma((CHUNKS,)),
        dma((CHUNKS,)),
        dma((CHUNKS,)),
        dma((CHUNKS,)),
        dma((CHUNKS,)),
        dma((CHUNKS,)),
        dma((CHUNKS,)),
    ]
    out = pl.pallas_call(
        kernel,
        out_shape=jax.ShapeDtypeStruct((tokens, 128), BF16),
        in_specs=[smem, smem] + [vmem] * 8,
        out_specs=vmem,
        scratch_shapes=scratch,
        compiler_params=pltpu.CompilerParams(
            collective_id=0, has_side_effects=True, vmem_limit_bytes=60 * 1024 * 1024
        ),
        name="prefill",
    )(
        images,
        texts,
        text_embed,
        patch,
        mw,
        bias.reshape(1, 128),
        gain,
        wq.reshape(NZ, NY, 2, 128, 128),
        jnp.swapaxes(wk[0], 0, 1),
        jnp.swapaxes(wv[0], 0, 1),
    )
    return out[None]


def solution(mesh):
    in_specs = (
        P(None, ("seq", "mp")),
        P(("section", "seq", "mp"), None),
        P(None, ("seq", "mp")),
        P(("seq", "mp")),
        P("section", None),
        P("section", None, ("seq", "mp")),
        P("section", None, ("seq", "mp")),
        P("section", None, ("seq", "mp")),
        P(),
        P(),
    )
    out_specs = P("section", None, ("seq", "mp"))
    return jax.shard_map(shards, mesh=mesh, in_specs=in_specs, out_specs=out_specs, check_vma=False)
```

```python
import functools
import math

import jax
import jax.numpy as jnp
from jax import lax
from jax.experimental import pallas as pl
from jax.experimental.pallas import tpu as pltpu
from jax.sharding import PartitionSpec as P

MESH = pl.DeviceIdType.MESH
F32 = jnp.float32
BF16 = jnp.bfloat16
HD = 128
NY = 4
NZ = 8
CHUNKS = 4
Z_ORDER = (4, 3, 5, 2, 6, 1, 7)


def iota(shape, dim):
    return lax.broadcasted_iota(jnp.int32, shape, dim)


def dot(a, b):
    return lax.dot_general(a, b, (((1,), (0,)), ((), ())), preferred_element_type=F32)


def dot_t(a, b):
    return lax.dot_general(a, b, (((1,), (1,)), ((), ())), preferred_element_type=F32)


def drain(ref, sem):
    pltpu.make_async_copy(ref, ref, sem).wait()


def kernel(
    images_ref,
    texts_ref,
    text_ref,
    patch_ref,
    mw_ref,
    bias_ref,
    gain_ref,
    wq_ref,
    wk_ref,
    wv_ref,
    out_ref,
    gains,
    actf,
    act,
    rows,
    rowsf,
    part,
    merged,
    start,
    kvtx,
    kvrx,
    kvrows,
    kvall,
    wq_own,
    wq_sib,
    mw_here,
    weights,
    states,
    xs,
    xr,
    kvx,
    spread,
    order,
    keys,
    values,
    l_wq,
    l_mw,
    s_act,
    r_act1,
    r_act2,
    r_act3,
    s_wq,
    r_wq,
    s_kv,
    r_kv,
    s_kvm,
    r_kvm,
    s_part,
    r_part,
    s_init,
    s_st,
    r_st,
    s_fw,
    r_fw,
    s_x,
    r_x,
    s_kx,
    r_kx,
):
    sec = lax.axis_index("section")
    seq = lax.axis_index("seq")
    core = lax.axis_index("mp")
    depth = lax.axis_size("section")
    z = seq // NY
    y = seq % NY
    tokens = out_ref.shape[0]
    tc = tokens // CHUNKS
    batch = tokens // images_ref.shape[0]
    per_batch = batch // tc

    def at_z(dz, s=None):
        return (sec if s is None else s, ((z + dz) % NZ) * NY + y, core)

    def at_y(dy):
        return (sec, z * NY + (y + dy) % NY, core)

    sibling = (sec, seq, 1 - core)

    def send(src, dst, ssem, rsem, device):
        pltpu.make_async_remote_copy(
            src_ref=src, dst_ref=dst, send_sem=ssem, recv_sem=rsem, device_id=device, device_id_type=MESH
        ).start()

    barrier = pltpu.get_barrier_semaphore()

    def greet(device):
        pl.semaphore_signal(barrier, inc=1, device_id=device, device_id_type=MESH)

    for dz in Z_ORDER:
        greet(at_z(dz))
    for dy in (2, 1, 3):
        greet(at_y(dy))
    greet(sibling)

    @pl.when(sec > 0)
    def _():
        for dz in (0,) + Z_ORDER:
            greet(at_z(dz, sec - 1))
        for dy in (2, 1, 3):
            greet((sec, z * NY + (y + dy) % NY, 1 - core))

    @pl.when(sec == 0)
    def _():
        for other in (1, 2, 3):
            greet((other, seq, core))

    load_wq = pltpu.make_async_copy(wq_ref, wq_own, l_wq)
    load_wq.start()
    load_mw = pltpu.make_async_copy(mw_ref, mw_here, l_mw)
    load_mw.start()
    for k in range(40):
        actf[k : k + 1, :] = patch_ref[:, k * 128 : (k + 1) * 128].astype(F32)
    xa = actf[...]
    act[...] = (0.5 * xa * (1.0 + lax.erf(xa * math.sqrt(0.5)))).astype(BF16)
    for k in range(64):
        gains[k : k + 1, :] = gain_ref[:, k * 128 : (k + 1) * 128].astype(F32)

    r_i, c_i = iota((128, 128), 0), iota((128, 128), 1)
    deal = (
        ((r_i >> 4) == (c_i & 7)) & (((r_i >> 2) & 3) == (c_i >> 5)) & ((r_i & 3) == ((c_i >> 3) & 3))
    )
    deal = jnp.where(deal, 1.0, 0.0).astype(BF16)
    for t in range(16):
        pieces = []
        for b in range(4):
            lanes = slice((4 * t + b) * 128, (4 * t + b + 1) * 128)
            pieces += [wk_ref[:, lanes], wv_ref[:, lanes]]
        kvtx[:, t] = dot(deal, jnp.concatenate(pieces, axis=0)).astype(BF16).reshape(NZ, 16, 128)
    r_i, c_i = iota((512, 256), 0), iota((512, 256), 1)
    lane = r_i & 127
    feature = 2 * ((lane & 7) * 8 + (r_i >> 7) * 2 + ((lane >> 5) & 1)) + ((lane >> 3) & 1)
    natural = (lane < 64) & (c_i == ((lane >> 4) & 1) * 128 + feature)
    spread[...] = jnp.where(natural, 1.0, 0.0).astype(BF16)
    r_i, c_i = iota((256, 256), 0), iota((256, 256), 1)
    feature = 2 * ((r_i & 7) * 8 + (r_i >> 5)) + ((r_i >> 3) & 1)
    order[...] = jnp.where(c_i == ((r_i >> 4) & 1) * 128 + feature, 1.0, 0.0).astype(BF16)

    def gain_of(q):
        g = gains[pl.ds(2 * q + core, 1), :]
        return jnp.where(iota((128, 128), 0) == iota((128, 128), 1), g, 0.0).astype(BF16)

    load_wq.wait()

    @pl.loop(0, NZ)
    def _(zz):
        for yy in range(NY):
            weights[zz, yy, :, 0:128] = dot(gain_of(zz * NY + yy), wq_own[zz, yy, core]).astype(BF16)

    @pl.when(sec == 0)
    def _():
        pl.semaphore_wait(barrier, 19)

    @pl.when((sec > 0) & (sec < depth - 1))
    def _():
        pl.semaphore_wait(barrier, 23)

    @pl.when(sec == depth - 1)
    def _():
        pl.semaphore_wait(barrier, 15)

    for dz in Z_ORDER:
        send(act, rows.at[core, z, y], s_act.at[0], r_act1, at_z(dz))
    pltpu.make_async_copy(act, rows.at[core, z, y], r_act1).start()
    send(wq_own.at[:, :, 1 - core], wq_sib, s_wq, r_wq, sibling)

    drain(rows.at[core, :, 0], r_act1)
    for i, dy in enumerate((2, 1, 3)):
        send(rows.at[core, :, y], rows.at[core, :, y], s_act.at[1], r_act2, at_y(dy))
    for dz in Z_ORDER:
        send(kvtx.at[(z + dz) % NZ], kvrx.at[z], s_kv, r_kv, at_z(dz))
    pltpu.make_async_copy(kvtx.at[z], kvrx.at[z], r_kv).start()

    drain(wq_sib, r_wq)

    @pl.loop(0, NZ)
    def _(zz):
        for yy in range(NY):
            weights[zz, yy, :, 128:256] = dot(gain_of(zz * NY + yy), wq_sib[zz, yy]).astype(BF16)

    drain(rows.at[core, :, pl.ds(0, 3)], r_act2)
    send(rows.at[core], rows.at[core], s_act.at[2], r_act3, sibling)
    drain(rows.at[core], r_act3)

    for p in range(2):
        for zz in range(NZ):
            for yy in range(NY):
                at = ((p * NZ + zz) * NY + yy) * 40
                rowsf[at : at + 40, :] = rows[p, zz, yy].astype(F32)
    load_mw.wait()
    acc = jnp.broadcast_to(bias_ref[...].astype(F32), (64, 128))
    for k in range(20):
        xk = jnp.concatenate(
            [rowsf[pl.ds(2 * k, 64, stride=40), :], rowsf[pl.ds(2 * k + 1, 64, stride=40), :]], axis=1
        ).astype(BF16)
        acc = acc + dot(xk, mw_here[256 * k : 256 * (k + 1), :])
    part[...] = acc.astype(BF16)

    @pl.when(sec == 1)
    def _():
        send(part, merged.at[1], s_part, r_part.at[0], (0, seq, core))

    @pl.when(sec > 1)
    def _():
        send(part, merged.at[sec], s_part, r_part.at[1], (0, seq, core))

    def place(rows_here, first):
        pos = first + iota((rows_here, 1), 0)
        begin = jnp.zeros((rows_here, 1), jnp.int32)
        count = jnp.zeros((rows_here, 1), jnp.int32)
        earlier = jnp.zeros((rows_here, 1), jnp.int32)
        at, seen = jnp.int32(0), jnp.int32(0)
        for b in range(images_ref.shape[0]):
            for r in range(images_ref.shape[1]):
                image, text = images_ref[b, r], texts_ref[b, r]
                inside = pos >= at
                begin = jnp.where(inside, at, begin)
                count = jnp.where(inside, image, count)
                earlier = jnp.where(inside, seen, earlier)
                at, seen = at + image + text, seen + image
        return pos, begin, count, earlier

    def begin_batch(m):
        first, count_here = m * batch, batch
        pos, begin, count, earlier = place(count_here, first)
        offset = pos - begin
        is_image = (offset >= 1) & (offset <= count)
        row = earlier + offset - 1 - m * 128
        slot = (row & 64) + ((row & 1) << 5) + ((row & 63) >> 1)
        chosen = (iota((count_here, 128), 1) == slot) & is_image
        picked = dot(
            jnp.where(chosen, 1.0, 0.0).astype(BF16), merged[2 * m : 2 * m + 2].reshape(128, 128)
        )
        text = text_ref[first : first + batch, :].astype(F32)
        start[first : first + batch, :] = jnp.where(is_image, picked, text).astype(BF16)
        for t in range(m * per_batch, (m + 1) * per_batch):
            src = start.at[pl.ds(t * tc, tc)]
            for dz in Z_ORDER:
                send(src, states.at[t, z, y], s_init.at[t], r_st.at[t], at_z(dz))
            pltpu.make_async_copy(src, states.at[t, z, y], r_st.at[t]).start()

    def forward(t):
        drain(states.at[t, :, 0], r_st.at[t])
        for dy in (2, 1, 3):
            send(states.at[t, :, y], states.at[t, :, y], s_fw.at[t], r_fw.at[t], at_y(dy))

    @pl.when(sec == 0)
    def _():
        merged[0] = part[...]
        drain(merged.at[1], r_part.at[0])
        begin_batch(0)
        drain(merged.at[pl.ds(2, 2)], r_part.at[1])
        begin_batch(1)

    drain(kvrx, r_kv)
    r_i, c_i = iota((128, 128), 0), iota((128, 128), 1)
    collect = ((r_i >> 5) == ((c_i >> 2) & 3)) & (((r_i >> 3) & 3) == (c_i & 3)) & ((r_i & 7) == (c_i >> 4))
    collect = jnp.where(collect, 1.0, 0.0).astype(BF16)
    for t in range(16):
        made = dot(collect, kvrx[:, t].reshape(128, 128)).astype(BF16).reshape(2, 2, 32, 128)
        for h in range(2):
            kvrows[t // 2, (t % 2) * 2 + h] = made[h]

    @pl.when(sec == 0)
    def _():
        send(kvrows.at[:, :, 1 - core], kvall.at[:, :, core], s_kvm, r_kvm, sibling)
        pltpu.make_async_copy(kvrows.at[:, :, core], kvall.at[:, :, core], r_kvm).start()
        forward(0)
        drain(kvall.at[:, :, pl.ds(0, 2)], r_kvm)

        @pl.loop(0, NZ)
        def _(zz):
            for yy in range(NY):
                mine = kvall[zz, yy, 0:2].reshape(64, 128)
                made = dot_t(gain_of(zz * NY + yy), mine)
                made = jnp.concatenate([made, jnp.zeros((128, 192), F32)], axis=1)
                weights[zz, yy, :, 256:512] = made.astype(BF16)

    @pl.when(sec > 0)
    def _():
        slot = 2 * y + core
        for dy in (2, 1, 3):
            for other in (core, 1 - core):
                to = (sec, z * NY + (y + dy) % NY, other)
                send(kvrows.at[:, :, other], kvall.at[:, :, slot], s_kvm, r_kvm, to)
        send(kvrows.at[:, :, 1 - core], kvall.at[:, :, slot], s_kvm, r_kvm, sibling)
        pltpu.make_async_copy(kvrows.at[:, :, core], kvall.at[:, :, slot], r_kvm).start()
        drain(kvall, r_kvm)

        @pl.loop(0, NZ)
        def _(zz):
            for yy in range(NY):
                made = dot_t(gain_of(zz * NY + yy), kvall[zz, yy].reshape(256, 128)).astype(BF16)
                weights[zz, yy, :, 256:512] = dot(made, order[...]).astype(BF16)

        forward(0)

    for t in range(CHUNKS):
        here = slice(t * tc, (t + 1) * tc)
        drain(states.at[t, :, pl.ds(0, 3)], r_fw.at[t])

        def products(zz, carry):
            acc, squares = carry
            x = jnp.concatenate([states[t, zz, yy] for yy in range(NY)], axis=1)
            acc = acc + dot(x, weights[zz].reshape(NY * 128, 512))
            xf = x.astype(F32)
            for yy in range(NY):
                piece = xf[:, yy * 128 : (yy + 1) * 128]
                squares = squares + piece * piece
            return acc, squares

        acc, squares = lax.fori_loop(
            0, NZ, products, (jnp.zeros((tc, 512), F32), jnp.zeros((tc, 128), F32)), unroll=2
        )
        total = jnp.broadcast_to(jnp.sum(squares, axis=1, keepdims=True), (tc, 128))
        own_q, own_kv = acc[:, 0:128], acc[:, 256:512]
        xs[t, :, 0:128] = acc[:, 128:256]
        xs[t, :, 128:384] = own_kv
        xs[t, :, 384:512] = total
        send(xs.at[t], xr.at[t], s_x.at[t], r_x.at[t], sibling)
        pos, begin, _, _ = place(tc, t * tc)

        if t + 1 < CHUNKS:

            @pl.when(sec > 0)
            def _():
                forward(t + 1)

        drain(xr.at[t], r_x.at[t])
        scale = lax.rsqrt((total + xr[t, :, 384:512]) * (1.0 / 8192.0) + 1e-6)
        scales = jnp.concatenate([scale, scale], axis=1)
        kv = ((own_kv + xr[t, :, 128:384]) * scales).astype(BF16)
        query = ((own_q + xr[t, :, 0:128]) * scale).astype(BF16)

        @pl.when(sec > 0)
        def _():
            keys[here, :] = kv[:, 0:128]
            values[here, :] = kv[:, 128:256]

        @pl.when(sec == 0)
        def _():
            kvx[t, y] = kv[:, 0:128]
            for dy in (2, 1, 3):
                send(kvx.at[t, y], kvx.at[t, y], s_kx.at[t], r_kx.at[t], at_y(dy))
            if t + 1 < CHUNKS:
                forward(t + 1)
            drain(kvx.at[t, pl.ds(0, 3)], r_kx.at[t])
            spread_kv = dot(jnp.concatenate([kvx[t, yy] for yy in range(NY)], axis=1), spread[...])
            keys[here, :] = spread_kv[:, 0:128].astype(BF16)
            values[here, :] = spread_kv[:, 128:256].astype(BF16)

        first = (t // per_batch) * batch
        span = (t % per_batch + 1) * tc
        column = first + iota((tc, span), 1)
        allowed = (column >= begin) & (column <= pos)
        scores = dot_t(query, keys[first : first + span, :]) * (1.0 / math.sqrt(HD))
        scores = jnp.where(allowed, scores, -1e30)
        weight = jnp.exp(scores - jnp.max(scores, axis=1, keepdims=True))
        probs = (weight / jnp.sum(weight, axis=1, keepdims=True)).astype(BF16)
        attended = dot(probs, values[first : first + span, :])
        state = states[t, z, y].astype(F32) + attended
        out_ref[t * tc : (t + 1) * tc, :] = state.astype(BF16)

        @pl.when(sec < depth - 1)
        def _():
            for dz in Z_ORDER + (0,):
                send(
                    out_ref.at[pl.ds(t * tc, tc)], states.at[t, z, y], s_st.at[t], r_st.at[t], at_z(dz, sec + 1)
                )

    drain(rows.at[core, pl.ds(0, 7), 0], s_act.at[0])
    drain(rows.at[core, :, pl.ds(0, 3)], s_act.at[1])
    drain(rows.at[core], s_act.at[2])
    drain(wq_sib, s_wq)
    drain(kvrx.at[pl.ds(0, 7)], s_kv)

    @pl.when(sec == 0)
    def _():
        drain(kvall.at[:, :, 0], s_kvm)

    @pl.when(sec > 0)
    def _():
        drain(part, s_part)
        drain(kvall.at[:, :, pl.ds(0, 7)], s_kvm)

    for t in range(CHUNKS):

        @pl.when(sec == 0)
        def _():
            drain(states.at[t, pl.ds(0, 7), 0], s_init.at[t])
            drain(kvx.at[t, pl.ds(0, 3)], s_kx.at[t])

        @pl.when(sec < depth - 1)
        def _():
            drain(states.at[t, :, 0], s_st.at[t])

        drain(states.at[t, :, pl.ds(0, 3)], s_fw.at[t])
        drain(xs.at[t], s_x.at[t])


def shards(text_embed, patch, mw, bias, gain, wq, wk, wv, images, texts):
    tokens = text_embed.shape[0]
    tc = tokens // CHUNKS
    vmem = pl.BlockSpec(memory_space=pltpu.VMEM)
    smem = pl.BlockSpec(memory_space=pltpu.SMEM)
    hbm = pl.BlockSpec(memory_space=pl.ANY)
    dma = pltpu.SemaphoreType.DMA
    scratch = [
        pltpu.VMEM((64, 128), F32),
        pltpu.VMEM((40, 128), F32),
        pltpu.VMEM((40, 128), BF16),
        pltpu.VMEM((2, NZ, NY, 40, 128), BF16),
        pltpu.VMEM((2560, 128), F32),
        pltpu.VMEM((64, 128), BF16),
        pltpu.VMEM((4, 64, 128), BF16),
        pltpu.VMEM((tokens, 128), BF16),
        pltpu.VMEM((NZ, 16, 16, 128), BF16),
        pltpu.VMEM((NZ, 16, 16, 128), BF16),
        pltpu.VMEM((NZ, NY, 2, 32, 128), BF16),
        pltpu.VMEM((NZ, NY, 8, 32, 128), BF16),
        pltpu.VMEM((NZ, NY, 2, 128, 128), BF16),
        pltpu.VMEM((NZ, NY, 128, 128), BF16),
        pltpu.VMEM(mw.shape, BF16),
        pltpu.VMEM((NZ, NY, 128, 512), BF16),
        pltpu.VMEM((CHUNKS, NZ, NY, tc, 128), BF16),
        pltpu.VMEM((CHUNKS, tc, 512), F32),
        pltpu.VMEM((CHUNKS, tc, 512), F32),
        pltpu.VMEM((CHUNKS, NY, tc, 128), BF16),
        pltpu.VMEM((512, 256), BF16),
        pltpu.VMEM((256, 256), BF16),
        pltpu.VMEM((tokens, 128), BF16),
        pltpu.VMEM((tokens, 128), BF16),
        dma,
        dma,
        dma((3,)),
        dma,
        dma,
        dma,
        dma,
        dma,
        dma,
        dma,
        dma,
        dma,
        dma,
        dma((2,)),
        dma((CHUNKS,)),
        dma((CHUNKS,)),
        dma((CHUNKS,)),
        dma((CHUNKS,)),
        dma((CHUNKS,)),
        dma((CHUNKS,)),
        dma((CHUNKS,)),
        dma((CHUNKS,)),
        dma((CHUNKS,)),
    ]
    out = pl.pallas_call(
        kernel,
        out_shape=jax.ShapeDtypeStruct((tokens, 128), BF16),
        in_specs=[smem, smem, vmem, vmem, hbm, vmem, vmem, hbm, vmem, vmem],
        out_specs=vmem,
        scratch_shapes=scratch,
        compiler_params=pltpu.CompilerParams(
            collective_id=0, has_side_effects=True, vmem_limit_bytes=60 * 1024 * 1024
        ),
        name="prefill",
    )(
        images,
        texts,
        text_embed,
        patch,
        mw,
        bias.reshape(1, 128),
        gain,
        wq.reshape(NZ, NY, 2, 128, 128),
        jnp.swapaxes(wk[0], 0, 1),
        jnp.swapaxes(wv[0], 0, 1),
    )
    return out[None]


def solution(mesh):
    in_specs = (
        P(None, ("seq", "mp")),
        P(("section", "seq", "mp"), None),
        P(None, ("seq", "mp")),
        P(("seq", "mp")),
        P("section", None),
        P("section", None, ("seq", "mp")),
        P("section", None, ("seq", "mp")),
        P("section", None, ("seq", "mp")),
        P(),
        P(),
    )
    out_specs = P("section", None, ("seq", "mp"))
    return jax.shard_map(shards, mesh=mesh, in_specs=in_specs, out_specs=out_specs, check_vma=False)
```

```python
import functools
import math

import jax
import jax.numpy as jnp
from jax import lax
from jax.experimental import pallas as pl
from jax.experimental.pallas import tpu as pltpu
from jax.sharding import PartitionSpec as P

MESH = pl.DeviceIdType.MESH
F32 = jnp.float32
BF16 = jnp.bfloat16
HD = 128
NY = 4
NZ = 8
CHUNKS = 4
Z_ORDER = (4, 3, 5, 2, 6, 1, 7)
CLASSES = ((0, 1, 7, 2), (6, 3, 5, 4))


def iota(shape, dim):
    return lax.broadcasted_iota(jnp.int32, shape, dim)


def dot(a, b):
    return lax.dot_general(a, b, (((1,), (0,)), ((), ())), preferred_element_type=F32)


def dot_t(a, b):
    return lax.dot_general(a, b, (((1,), (1,)), ((), ())), preferred_element_type=F32)


def drain(ref, sem):
    pltpu.make_async_copy(ref, ref, sem).wait()


def kernel(
    images_ref,
    texts_ref,
    text_ref,
    patch_ref,
    mw_ref,
    bias_ref,
    gain_ref,
    wq_ref,
    wk_ref,
    wv_ref,
    out_ref,
    gains,
    actf,
    act,
    rows,
    rowsf,
    part,
    merged,
    start,
    kvtx,
    kvrx,
    kvrows,
    kvall,
    wq_own,
    wq_sib,
    mw_here,
    weights,
    states,
    xs,
    xr,
    kvx,
    spread,
    order,
    queries,
    keys,
    values,
    l_wq,
    l_mw,
    s_act,
    r_act1,
    r_act2,
    r_act3,
    s_wq,
    r_wq,
    s_kv,
    r_kv,
    s_kvm,
    r_kvm,
    r_kvn,
    r_kvf,
    s_part,
    r_part,
    s_init,
    s_st,
    r_st,
    s_fw,
    r_near,
    r_far,
    s_x,
    r_x,
    s_kx,
    r_kx,
):
    sec = lax.axis_index("section")
    seq = lax.axis_index("seq")
    core = lax.axis_index("mp")
    depth = lax.axis_size("section")
    z = seq // NY
    y = seq % NY
    tokens = out_ref.shape[0]
    tc = tokens // CHUNKS
    batch = tokens // images_ref.shape[0]

    def at_z(dz, s=None):
        return (sec if s is None else s, ((z + dz) % NZ) * NY + y, core)

    def at_y(dy):
        return (sec, z * NY + (y + dy) % NY, core)

    sibling = (sec, seq, 1 - core)

    def send(src, dst, ssem, rsem, device):
        pltpu.make_async_remote_copy(
            src_ref=src, dst_ref=dst, send_sem=ssem, recv_sem=rsem, device_id=device, device_id_type=MESH
        ).start()

    barrier = pltpu.get_barrier_semaphore()

    def greet(device):
        pl.semaphore_signal(barrier, inc=1, device_id=device, device_id_type=MESH)

    for dz in Z_ORDER:
        greet(at_z(dz))
    for dy in (2, 1, 3):
        greet(at_y(dy))
    greet(sibling)

    @pl.when(sec > 0)
    def _():
        for dz in (0,) + Z_ORDER:
            greet(at_z(dz, sec - 1))
        for dy in (1, 3):
            greet((sec, z * NY + (y + dy) % NY, 1 - core))

    @pl.when(sec == 0)
    def _():
        for other in (1, 2, 3):
            greet((other, seq, core))

    load_wq = pltpu.make_async_copy(wq_ref, wq_own, l_wq)
    load_wq.start()
    load_mw = pltpu.make_async_copy(mw_ref, mw_here, l_mw)
    load_mw.start()
    for k in range(40):
        actf[k : k + 1, :] = patch_ref[:, k * 128 : (k + 1) * 128].astype(F32)
    xa = actf[...]
    act[...] = (0.5 * xa * (1.0 + lax.erf(xa * math.sqrt(0.5)))).astype(BF16)
    for k in range(64):
        gains[k : k + 1, :] = gain_ref[:, k * 128 : (k + 1) * 128].astype(F32)

    r_i, c_i = iota((128, 128), 0), iota((128, 128), 1)
    deal = (
        ((r_i >> 4) == (c_i & 7)) & (((r_i >> 2) & 3) == (c_i >> 5)) & ((r_i & 3) == ((c_i >> 3) & 3))
    )
    deal = jnp.where(deal, 1.0, 0.0).astype(BF16)
    for t in range(16):
        pieces = []
        for b in range(4):
            lanes = slice((4 * t + b) * 128, (4 * t + b + 1) * 128)
            pieces += [wk_ref[:, lanes], wv_ref[:, lanes]]
        kvtx[:, t] = dot(deal, jnp.concatenate(pieces, axis=0)).astype(BF16).reshape(NZ, 16, 128)
    r_i, c_i = iota((512, 256), 0), iota((512, 256), 1)
    lane = r_i & 127
    feature = 2 * ((lane & 7) * 8 + (r_i >> 7) * 2 + ((lane >> 5) & 1)) + ((lane >> 3) & 1)
    natural = (lane < 64) & (c_i == ((lane >> 4) & 1) * 128 + feature)
    spread[...] = jnp.where(natural, 1.0, 0.0).astype(BF16)
    r_i, c_i = iota((256, 256), 0), iota((256, 256), 1)
    feature = 2 * ((r_i & 7) * 8 + (r_i >> 5)) + ((r_i >> 3) & 1)
    order[...] = jnp.where(c_i == ((r_i >> 4) & 1) * 128 + feature, 1.0, 0.0).astype(BF16)

    def gain_of(q):
        g = gains[pl.ds(2 * q + core, 1), :]
        return jnp.where(iota((128, 128), 0) == iota((128, 128), 1), g, 0.0).astype(BF16)

    load_wq.wait()

    @pl.loop(0, NZ)
    def _(zz):
        for yy in range(NY):
            weights[zz, yy, :, 0:128] = dot(gain_of(zz * NY + yy), wq_own[zz, yy, core]).astype(BF16)

    @pl.when(sec == 0)
    def _():
        pl.semaphore_wait(barrier, 19)

    @pl.when((sec > 0) & (sec < depth - 1))
    def _():
        pl.semaphore_wait(barrier, 22)

    @pl.when(sec == depth - 1)
    def _():
        pl.semaphore_wait(barrier, 14)

    for dz in Z_ORDER:
        send(act, rows.at[core, z, y], s_act.at[0], r_act1, at_z(dz))
    pltpu.make_async_copy(act, rows.at[core, z, y], r_act1).start()

    def deal_rows():
        for dz in Z_ORDER:
            send(kvtx.at[(z + dz) % NZ], kvrx.at[z], s_kv, r_kv, at_z(dz))
        pltpu.make_async_copy(kvtx.at[z], kvrx.at[z], r_kv).start()

    send(wq_own.at[:, :, 1 - core], wq_sib, s_wq, r_wq, sibling)

    drain(rows.at[core, :, 0], r_act1)
    for i, dy in enumerate((2, 1, 3)):
        send(rows.at[core, :, y], rows.at[core, :, y], s_act.at[1], r_act2, at_y(dy))
    deal_rows()

    drain(wq_sib, r_wq)

    @pl.loop(0, NZ)
    def _(zz):
        for yy in range(NY):
            weights[zz, yy, :, 128:256] = dot(gain_of(zz * NY + yy), wq_sib[zz, yy]).astype(BF16)

    drain(rows.at[core, :, pl.ds(0, 3)], r_act2)
    send(rows.at[core], rows.at[core], s_act.at[2], r_act3, sibling)
    drain(rows.at[core], r_act3)

    for p in range(2):
        for zz in range(NZ):
            for yy in range(NY):
                at = ((p * NZ + zz) * NY + yy) * 40
                rowsf[at : at + 40, :] = rows[p, zz, yy].astype(F32)
    load_mw.wait()
    acc = jnp.broadcast_to(bias_ref[...].astype(F32), (64, 128))
    for k in range(20):
        xk = jnp.concatenate(
            [rowsf[pl.ds(2 * k, 64, stride=40), :], rowsf[pl.ds(2 * k + 1, 64, stride=40), :]], axis=1
        ).astype(BF16)
        acc = acc + dot(xk, mw_here[256 * k : 256 * (k + 1), :])
    part[...] = acc.astype(BF16)

    @pl.when(sec == 1)
    def _():
        send(part, merged.at[1], s_part, r_part.at[0], (0, seq, core))

    @pl.when(sec > 1)
    def _():
        send(part, merged.at[sec], s_part, r_part.at[1], (0, seq, core))

    def place(rows_here, first):
        pos = first + iota((rows_here, 1), 0)
        begin = jnp.zeros((rows_here, 1), jnp.int32)
        count = jnp.zeros((rows_here, 1), jnp.int32)
        earlier = jnp.zeros((rows_here, 1), jnp.int32)
        at, seen = jnp.int32(0), jnp.int32(0)
        for b in range(images_ref.shape[0]):
            for r in range(images_ref.shape[1]):
                image, text = images_ref[b, r], texts_ref[b, r]
                inside = pos >= at
                begin = jnp.where(inside, at, begin)
                count = jnp.where(inside, image, count)
                earlier = jnp.where(inside, seen, earlier)
                at, seen = at + image + text, seen + image
        return pos, begin, count, earlier

    def begin_batch(m):
        first, count_here = m * batch, batch
        pos, begin, count, earlier = place(count_here, first)
        offset = pos - begin
        is_image = (offset >= 1) & (offset <= count)
        row = earlier + offset - 1 - m * 128
        slot = (row & 64) + ((row & 1) << 5) + ((row & 63) >> 1)
        chosen = (iota((count_here, 128), 1) == slot) & is_image
        picked = dot(
            jnp.where(chosen, 1.0, 0.0).astype(BF16), merged[2 * m : 2 * m + 2].reshape(128, 128)
        )
        text = text_ref[first : first + batch, :].astype(F32)
        start[first : first + batch, :] = jnp.where(is_image, picked, text).astype(BF16)

    def begin_chunk(t):
        src = start.at[pl.ds(t * tc, tc)]
        for k in range(2):
            for dz in CLASSES[k]:
                if dz:
                    send(src, states.at[t, z, y], s_init.at[t], r_st.at[t, k], at_z(dz))
        pltpu.make_async_copy(src, states.at[t, z, y], r_st.at[t, 0]).start()

    def from_z(t, dz, yy):
        return states.at[t, (z + NZ - dz) % NZ, yy % NY]

    def forward(t):
        for k in range(2):
            drain(states.at[t, pl.ds(0, 4), 0], r_st.at[t, k])
            for dz in CLASSES[k]:
                block = from_z(t, dz, y)
                send(block, block, s_fw.at[t], r_near.at[t, k, 0], at_y(1))
                send(block, block, s_fw.at[t], r_near.at[t, k, 1], at_y(3))

    def pass_on(t):
        for k in range(2):
            drain(states.at[t, pl.ds(0, 4), 0], r_near.at[t, k, 0])
            for dz in CLASSES[k][:2]:
                block = from_z(t, dz, y + 3)
                send(block, block, s_fw.at[t], r_far.at[t], at_y(1))
            drain(states.at[t, pl.ds(0, 4), 0], r_near.at[t, k, 1])
            for dz in CLASSES[k][2:]:
                block = from_z(t, dz, y + 1)
                send(block, block, s_fw.at[t], r_far.at[t], at_y(3))

    @pl.when(sec == 0)
    def _():
        merged[0] = part[...]
        drain(merged.at[1], r_part.at[0])
        begin_batch(0)
        begin_chunk(0)
        drain(merged.at[pl.ds(2, 2)], r_part.at[1])
        begin_batch(1)

    drain(kvrx, r_kv)
    r_i, c_i = iota((128, 128), 0), iota((128, 128), 1)
    collect = ((r_i >> 5) == ((c_i >> 2) & 3)) & (((r_i >> 3) & 3) == (c_i & 3)) & ((r_i & 7) == (c_i >> 4))
    collect = jnp.where(collect, 1.0, 0.0).astype(BF16)
    for t in range(16):
        made = dot(collect, kvrx[:, t].reshape(128, 128)).astype(BF16).reshape(2, 2, 32, 128)
        for h in range(2):
            kvrows[t // 2, (t % 2) * 2 + h] = made[h]

    @pl.when(sec == 0)
    def _():
        send(kvrows.at[:, :, 1 - core], kvall.at[:, :, core], s_kvm, r_kvm, sibling)
        pltpu.make_async_copy(kvrows.at[:, :, core], kvall.at[:, :, core], r_kvm).start()
        forward(0)
        begin_chunk(1)
        drain(kvall.at[:, :, pl.ds(0, 2)], r_kvm)

        @pl.loop(0, NZ)
        def _(zz):
            for yy in range(NY):
                mine = kvall[zz, yy, 0:2].reshape(64, 128)
                made = dot_t(gain_of(zz * NY + yy), mine)
                made = jnp.concatenate([made, jnp.zeros((128, 192), F32)], axis=1)
                weights[zz, yy, :, 256:512] = made.astype(BF16)

    @pl.when(sec > 0)
    def _():
        slot = 2 * y + core
        for i, dy in enumerate((1, 3)):
            for other in (core, 1 - core):
                to = (sec, z * NY + (y + dy) % NY, other)
                send(kvrows.at[:, :, other], kvall.at[:, :, slot], s_kvm, r_kvn.at[i], to)
        send(kvrows.at[:, :, 1 - core], kvall.at[:, :, slot], s_kvm, r_kvm, sibling)
        pltpu.make_async_copy(kvrows.at[:, :, core], kvall.at[:, :, slot], r_kvm).start()
        drain(kvall.at[:, :, pl.ds(0, 2)], r_kvn.at[0])
        below = kvall.at[:, :, 2 * ((y + 3) % NY) + 1]
        send(below, below, s_kvm, r_kvf, at_y(1))
        drain(kvall.at[:, :, pl.ds(0, 2)], r_kvn.at[1])
        above = kvall.at[:, :, 2 * ((y + 1) % NY)]
        send(above, above, s_kvm, r_kvf, at_y(3))
        drain(kvall.at[:, :, pl.ds(0, 2)], r_kvm)
        drain(kvall.at[:, :, pl.ds(0, 2)], r_kvf)

        @pl.loop(0, NZ)
        def _(zz):
            for yy in range(NY):
                made = dot_t(gain_of(zz * NY + yy), kvall[zz, yy].reshape(256, 128)).astype(BF16)
                weights[zz, yy, :, 256:512] = dot(made, order[...]).astype(BF16)

        forward(0)

    def project(t):
        def products(zz, carry):
            acc, squares = carry
            x = jnp.concatenate([states[t, zz, yy] for yy in range(NY)], axis=1)
            acc = acc + dot(x, weights[zz].reshape(NY * 128, 512))
            xf = x.astype(F32)
            for yy in range(NY):
                piece = xf[:, yy * 128 : (yy + 1) * 128]
                squares = squares + piece * piece
            return acc, squares

        acc, squares = lax.fori_loop(
            0, NZ, products, (jnp.zeros((tc, 512), F32), jnp.zeros((tc, 128), F32)), unroll=2
        )
        total = jnp.broadcast_to(jnp.sum(squares, axis=1, keepdims=True), (tc, 128))
        own_q, own_kv = acc[:, 0:128], acc[:, 256:512]
        xs[t, :, 0:128] = acc[:, 128:256]
        xs[t, :, 128:384] = own_kv
        xs[t, :, 384:512] = total
        send(xs.at[t], xr.at[t], s_x.at[t], r_x.at[t], sibling)
        drain(xr.at[t], r_x.at[t])
        scale = lax.rsqrt((total + xr[t, :, 384:512]) * (1.0 / 8192.0) + 1e-6)
        scales = jnp.concatenate([scale, scale], axis=1)
        kv = ((own_kv + xr[t, :, 128:384]) * scales).astype(BF16)
        queries[t] = ((own_q + xr[t, :, 0:128]) * scale).astype(BF16)
        return kv

    def attend(t):
        here = slice(t * tc, (t + 1) * tc)
        first = (t * tc // batch) * batch
        span = (t + 1) * tc - first
        pos, begin, _, _ = place(tc, t * tc)
        column = first + iota((tc, span), 1)
        allowed = (column >= begin) & (column <= pos)
        scores = dot_t(queries[t], keys[first : first + span, :]) * (1.0 / math.sqrt(HD))
        scores = jnp.where(allowed, scores, -1e30)
        weight = jnp.exp(scores - jnp.max(scores, axis=1, keepdims=True))
        probs = (weight / jnp.sum(weight, axis=1, keepdims=True)).astype(BF16)
        attended = dot(probs, values[first : first + span, :])
        state = states[t, z, y].astype(F32) + attended
        out_ref[here, :] = state.astype(BF16)

        @pl.when(sec < depth - 1)
        def _():
            for k in range(2):
                for dz in CLASSES[k]:
                    send(
                        out_ref.at[pl.ds(t * tc, tc)],
                        states.at[t, z, y],
                        s_st.at[t],
                        r_st.at[t, k],
                        at_z(dz, sec + 1),
                    )

    def attend_shared(t):
        here = slice(t * tc, (t + 1) * tc)
        drain(kvx.at[t, pl.ds(0, 3)], r_kx.at[t])
        kv = dot(jnp.concatenate([kvx[t, yy] for yy in range(NY)], axis=1), spread[...]).astype(BF16)
        keys[here, :] = kv[:, 0:128]
        values[here, :] = kv[:, 128:256]
        attend(t)

    @pl.when(sec == 0)
    def _():
        def next_chunk(t):
            if t < CHUNKS:
                forward(t)
            if t + 1 < CHUNKS:
                begin_chunk(t + 1)

        pass_on(0)
        next_chunk(1)
        for t in range(CHUNKS):
            drain(states.at[t, :, 0], r_far.at[t])
            kv = project(t)
            kvx[t, y] = kv[:, 0:128]
            for dy in (2, 1, 3):
                send(kvx.at[t, y], kvx.at[t, y], s_kx.at[t], r_kx.at[t], at_y(dy))
            if t + 1 < CHUNKS:
                pass_on(t + 1)
            next_chunk(t + 2)
            attend_shared(t)

    @pl.when(sec > 0)
    def _():
        for t in range(CHUNKS):
            here = slice(t * tc, (t + 1) * tc)
            pass_on(t)
            if t + 1 < CHUNKS:
                forward(t + 1)
            drain(states.at[t, :, 0], r_far.at[t])
            kv = project(t)
            keys[here, :] = kv[:, 0:128]
            values[here, :] = kv[:, 128:256]
            attend(t)

    drain(rows.at[core, pl.ds(0, 7), 0], s_act.at[0])
    drain(rows.at[core, :, pl.ds(0, 3)], s_act.at[1])
    drain(rows.at[core], s_act.at[2])
    drain(wq_sib, s_wq)
    drain(kvrx.at[pl.ds(0, 7)], s_kv)

    @pl.when(sec == 0)
    def _():
        drain(kvall.at[:, :, 0], s_kvm)

    @pl.when(sec > 0)
    def _():
        drain(part, s_part)
        drain(kvall.at[:, :, pl.ds(0, 7)], s_kvm)

    for t in range(CHUNKS):

        @pl.when(sec == 0)
        def _():
            drain(states.at[t, pl.ds(0, 7), 0], s_init.at[t])
            drain(kvx.at[t, pl.ds(0, 3)], s_kx.at[t])

        @pl.when(sec < depth - 1)
        def _():
            drain(states.at[t, :, 0], s_st.at[t])

        drain(states.at[t, :, pl.ds(0, 3)], s_fw.at[t])
        drain(xs.at[t], s_x.at[t])


def shards(text_embed, patch, mw, bias, gain, wq, wk, wv, images, texts):
    tokens = text_embed.shape[0]
    tc = tokens // CHUNKS
    vmem = pl.BlockSpec(memory_space=pltpu.VMEM)
    smem = pl.BlockSpec(memory_space=pltpu.SMEM)
    hbm = pl.BlockSpec(memory_space=pl.ANY)
    dma = pltpu.SemaphoreType.DMA
    scratch = [
        pltpu.VMEM((64, 128), F32),
        pltpu.VMEM((40, 128), F32),
        pltpu.VMEM((40, 128), BF16),
        pltpu.VMEM((2, NZ, NY, 40, 128), BF16),
        pltpu.VMEM((2560, 128), F32),
        pltpu.VMEM((64, 128), BF16),
        pltpu.VMEM((4, 64, 128), BF16),
        pltpu.VMEM((tokens, 128), BF16),
        pltpu.VMEM((NZ, 16, 16, 128), BF16),
        pltpu.VMEM((NZ, 16, 16, 128), BF16),
        pltpu.VMEM((NZ, NY, 2, 32, 128), BF16),
        pltpu.VMEM((NZ, NY, 8, 32, 128), BF16),
        pltpu.VMEM((NZ, NY, 2, 128, 128), BF16),
        pltpu.VMEM((NZ, NY, 128, 128), BF16),
        pltpu.VMEM(mw.shape, BF16),
        pltpu.VMEM((NZ, NY, 128, 512), BF16),
        pltpu.VMEM((CHUNKS, NZ, NY, tc, 128), BF16),
        pltpu.VMEM((CHUNKS, tc, 512), F32),
        pltpu.VMEM((CHUNKS, tc, 512), F32),
        pltpu.VMEM((CHUNKS, NY, tc, 128), BF16),
        pltpu.VMEM((512, 256), BF16),
        pltpu.VMEM((256, 256), BF16),
        pltpu.VMEM((CHUNKS, tc, 128), BF16),
        pltpu.VMEM((tokens, 128), BF16),
        pltpu.VMEM((tokens, 128), BF16),
        dma,
        dma,
        dma((3,)),
        dma,
        dma,
        dma,
        dma,
        dma,
        dma,
        dma,
        dma,
        dma,
        dma((2,)),
        dma,
        dma,
        dma((2,)),
        dma((CHUNKS,)),
        dma((CHUNKS,)),
        dma((CHUNKS, 2)),
        dma((CHUNKS,)),
        dma((CHUNKS, 2, 2)),
        dma((CHUNKS,)),
        dma((CHUNKS,)),
        dma((CHUNKS,)),
        dma((CHUNKS,)),
        dma((CHUNKS,)),
    ]
    out = pl.pallas_call(
        kernel,
        out_shape=jax.ShapeDtypeStruct((tokens, 128), BF16),
        in_specs=[smem, smem, vmem, vmem, hbm, vmem, vmem, hbm, vmem, vmem],
        out_specs=vmem,
        scratch_shapes=scratch,
        compiler_params=pltpu.CompilerParams(
            collective_id=0, has_side_effects=True, vmem_limit_bytes=60 * 1024 * 1024
        ),
        name="prefill",
    )(
        images,
        texts,
        text_embed,
        patch,
        mw,
        bias.reshape(1, 128),
        gain,
        wq.reshape(NZ, NY, 2, 128, 128),
        jnp.swapaxes(wk[0], 0, 1),
        jnp.swapaxes(wv[0], 0, 1),
    )
    return out[None]


def solution(mesh):
    in_specs = (
        P(None, ("seq", "mp")),
        P(("section", "seq", "mp"), None),
        P(None, ("seq", "mp")),
        P(("seq", "mp")),
        P("section", None),
        P("section", None, ("seq", "mp")),
        P("section", None, ("seq", "mp")),
        P("section", None, ("seq", "mp")),
        P(),
        P(),
    )
    out_specs = P("section", None, ("seq", "mp"))
    return jax.shard_map(shards, mesh=mesh, in_specs=in_specs, out_specs=out_specs, check_vma=False)
```

```python
import functools
import math

import jax
import jax.numpy as jnp
from jax import lax
from jax.experimental import pallas as pl
from jax.experimental.pallas import tpu as pltpu
from jax.sharding import PartitionSpec as P

MESH = pl.DeviceIdType.MESH
F32 = jnp.float32
BF16 = jnp.bfloat16
HD = 128
NY = 4
NZ = 8
CHUNKS = 4
Z_ORDER = (4, 3, 5, 2, 6, 1, 7)
KINDS = 4
PER_KIND = NZ // KINDS
VISIT = (0, 1, 3, 2)
SENDS = (0, 7, 1, 2, 6, 5, 3, 4)


def iota(shape, dim):
    return lax.broadcasted_iota(jnp.int32, shape, dim)


def dot(a, b):
    return lax.dot_general(a, b, (((1,), (0,)), ((), ())), preferred_element_type=F32)


def dot_t(a, b):
    return lax.dot_general(a, b, (((1,), (1,)), ((), ())), preferred_element_type=F32)


def drain(ref, sem):
    pltpu.make_async_copy(ref, ref, sem).wait()


def kernel(
    images_ref,
    texts_ref,
    text_ref,
    patch_ref,
    mw_ref,
    bias_ref,
    gain_ref,
    wq_ref,
    wk_ref,
    wv_ref,
    out_ref,
    gains,
    actf,
    act,
    rows,
    rowsf,
    part,
    merged,
    start,
    kvtx,
    kvrx,
    kvrows,
    kvall,
    wq_own,
    wq_sib,
    mw_here,
    weights,
    states,
    xs,
    xr,
    kvx,
    spread,
    order,
    queries,
    keys,
    values,
    l_wq,
    l_mw,
    s_act,
    r_act1,
    r_act2,
    r_act3,
    s_wq,
    r_wq,
    s_kv,
    r_kv,
    s_kvm,
    r_kvm,
    r_kvn,
    r_kvf,
    s_part,
    r_part,
    s_init,
    s_st,
    r_st,
    s_fw,
    r_near,
    r_far,
    s_x,
    r_x,
    s_kx,
    r_kx,
):
    sec = lax.axis_index("section")
    seq = lax.axis_index("seq")
    core = lax.axis_index("mp")
    depth = lax.axis_size("section")
    z = seq // NY
    y = seq % NY
    tokens = out_ref.shape[0]
    tc = tokens // CHUNKS
    batch = tokens // images_ref.shape[0]

    def at_z(dz, s=None):
        return (sec if s is None else s, ((z + dz) % NZ) * NY + y, core)

    def at_y(dy):
        return (sec, z * NY + (y + dy) % NY, core)

    sibling = (sec, seq, 1 - core)

    def send(src, dst, ssem, rsem, device):
        pltpu.make_async_remote_copy(
            src_ref=src, dst_ref=dst, send_sem=ssem, recv_sem=rsem, device_id=device, device_id_type=MESH
        ).start()

    barrier = pltpu.get_barrier_semaphore()

    def greet(device):
        pl.semaphore_signal(barrier, inc=1, device_id=device, device_id_type=MESH)

    for dz in Z_ORDER:
        greet(at_z(dz))
    for dy in (2, 1, 3):
        greet(at_y(dy))
    greet(sibling)

    @pl.when(sec > 0)
    def _():
        for dz in (0,) + Z_ORDER:
            greet(at_z(dz, sec - 1))
        for dy in (1, 3):
            greet((sec, z * NY + (y + dy) % NY, 1 - core))

    @pl.when(sec == 0)
    def _():
        for other in (1, 2, 3):
            greet((other, seq, core))

    load_wq = pltpu.make_async_copy(wq_ref, wq_own, l_wq)
    load_wq.start()
    load_mw = pltpu.make_async_copy(mw_ref, mw_here, l_mw)
    load_mw.start()
    for k in range(40):
        actf[k : k + 1, :] = patch_ref[:, k * 128 : (k + 1) * 128].astype(F32)
    xa = actf[...]
    act[...] = (0.5 * xa * (1.0 + lax.erf(xa * math.sqrt(0.5)))).astype(BF16)
    for k in range(64):
        gains[k : k + 1, :] = gain_ref[:, k * 128 : (k + 1) * 128].astype(F32)

    r_i, c_i = iota((128, 128), 0), iota((128, 128), 1)
    deal = (
        ((r_i >> 4) == (c_i & 7)) & (((r_i >> 2) & 3) == (c_i >> 5)) & ((r_i & 3) == ((c_i >> 3) & 3))
    )
    deal = jnp.where(deal, 1.0, 0.0).astype(BF16)
    for t in range(16):
        pieces = []
        for b in range(4):
            lanes = slice((4 * t + b) * 128, (4 * t + b + 1) * 128)
            pieces += [wk_ref[:, lanes], wv_ref[:, lanes]]
        kvtx[:, t] = dot(deal, jnp.concatenate(pieces, axis=0)).astype(BF16).reshape(NZ, 16, 128)
    r_i, c_i = iota((512, 256), 0), iota((512, 256), 1)
    lane = r_i & 127
    feature = 2 * ((lane & 7) * 8 + (r_i >> 7) * 2 + ((lane >> 5) & 1)) + ((lane >> 3) & 1)
    natural = (lane < 64) & (c_i == ((lane >> 4) & 1) * 128 + feature)
    spread[...] = jnp.where(natural, 1.0, 0.0).astype(BF16)
    r_i, c_i = iota((256, 256), 0), iota((256, 256), 1)
    feature = 2 * ((r_i & 7) * 8 + (r_i >> 5)) + ((r_i >> 3) & 1)
    order[...] = jnp.where(c_i == ((r_i >> 4) & 1) * 128 + feature, 1.0, 0.0).astype(BF16)

    def gain_of(q):
        g = gains[pl.ds(2 * q + core, 1), :]
        return jnp.where(iota((128, 128), 0) == iota((128, 128), 1), g, 0.0).astype(BF16)

    load_wq.wait()

    @pl.loop(0, NZ)
    def _(zz):
        for yy in range(NY):
            weights[zz, yy, :, 0:128] = dot(gain_of(zz * NY + yy), wq_own[zz, yy, core]).astype(BF16)

    @pl.when(sec == 0)
    def _():
        pl.semaphore_wait(barrier, 19)

    @pl.when((sec > 0) & (sec < depth - 1))
    def _():
        pl.semaphore_wait(barrier, 22)

    @pl.when(sec == depth - 1)
    def _():
        pl.semaphore_wait(barrier, 14)

    for dz in Z_ORDER:
        send(act, rows.at[core, z, y], s_act.at[0], r_act1, at_z(dz))
    pltpu.make_async_copy(act, rows.at[core, z, y], r_act1).start()

    def deal_rows():
        for dz in Z_ORDER:
            send(kvtx.at[(z + dz) % NZ], kvrx.at[z], s_kv, r_kv, at_z(dz))
        pltpu.make_async_copy(kvtx.at[z], kvrx.at[z], r_kv).start()


    @pl.when(sec == 0)
    def _():
        deal_rows()

    send(wq_own.at[:, :, 1 - core], wq_sib, s_wq, r_wq, sibling)

    drain(rows.at[core, :, 0], r_act1)
    for i, dy in enumerate((2, 1, 3)):
        send(rows.at[core, :, y], rows.at[core, :, y], s_act.at[1], r_act2, at_y(dy))

    @pl.when(sec > 0)
    def _():
        deal_rows()

    drain(wq_sib, r_wq)

    @pl.loop(0, NZ)
    def _(zz):
        for yy in range(NY):
            weights[zz, yy, :, 128:256] = dot(gain_of(zz * NY + yy), wq_sib[zz, yy]).astype(BF16)

    drain(rows.at[core, :, pl.ds(0, 3)], r_act2)
    send(rows.at[core], rows.at[core], s_act.at[2], r_act3, sibling)
    drain(rows.at[core], r_act3)

    for p in range(2):
        for zz in range(NZ):
            for yy in range(NY):
                at = ((p * NZ + zz) * NY + yy) * 40
                rowsf[at : at + 40, :] = rows[p, zz, yy].astype(F32)
    load_mw.wait()
    acc = jnp.broadcast_to(bias_ref[...].astype(F32), (64, 128))
    for k in range(20):
        xk = jnp.concatenate(
            [rowsf[pl.ds(2 * k, 64, stride=40), :], rowsf[pl.ds(2 * k + 1, 64, stride=40), :]], axis=1
        ).astype(BF16)
        acc = acc + dot(xk, mw_here[256 * k : 256 * (k + 1), :])
    part[...] = acc.astype(BF16)

    @pl.when(sec == 1)
    def _():
        send(part, merged.at[1], s_part, r_part.at[0], (0, seq, core))

    @pl.when(sec > 1)
    def _():
        send(part, merged.at[sec], s_part, r_part.at[1], (0, seq, core))

    def place(rows_here, first):
        pos = first + iota((rows_here, 1), 0)
        begin = jnp.zeros((rows_here, 1), jnp.int32)
        count = jnp.zeros((rows_here, 1), jnp.int32)
        earlier = jnp.zeros((rows_here, 1), jnp.int32)
        at, seen = jnp.int32(0), jnp.int32(0)
        for b in range(images_ref.shape[0]):
            for r in range(images_ref.shape[1]):
                image, text = images_ref[b, r], texts_ref[b, r]
                inside = pos >= at
                begin = jnp.where(inside, at, begin)
                count = jnp.where(inside, image, count)
                earlier = jnp.where(inside, seen, earlier)
                at, seen = at + image + text, seen + image
        return pos, begin, count, earlier

    def begin_batch(m):
        first, count_here = m * batch, batch
        pos, begin, count, earlier = place(count_here, first)
        offset = pos - begin
        is_image = (offset >= 1) & (offset <= count)
        row = earlier + offset - 1 - m * 128
        slot = (row & 64) + ((row & 1) << 5) + ((row & 63) >> 1)
        chosen = (iota((count_here, 128), 1) == slot) & is_image
        picked = dot(
            jnp.where(chosen, 1.0, 0.0).astype(BF16), merged[2 * m : 2 * m + 2].reshape(128, 128)
        )
        text = text_ref[first : first + batch, :].astype(F32)
        start[first : first + batch, :] = jnp.where(is_image, picked, text).astype(BF16)

    def slot_of(dz):
        return (dz + 1) % NZ

    def begin_chunk(t):
        src = start.at[pl.ds(t * tc, tc)]
        for dz in SENDS:
            if dz:
                send(src, states.at[t, y, slot_of(dz)], s_init.at[t], r_st.at[t, slot_of(dz) // PER_KIND], at_z(dz))
        pltpu.make_async_copy(src, states.at[t, y, slot_of(0)], r_st.at[t, slot_of(0) // PER_KIND]).start()

    def forward(t, i):
        k = VISIT[i]
        drain(states.at[t, 0, pl.ds(0, PER_KIND)], r_st.at[t, k])
        block = states.at[t, y, pl.ds(k * PER_KIND, PER_KIND)]
        send(block, block, s_fw.at[t], r_near.at[t, k, 0], at_y(1))
        send(block, block, s_fw.at[t], r_near.at[t, k, 1], at_y(3))

    def pass_on(t, i):
        k, half = VISIT[i], PER_KIND // 2
        drain(states.at[t, 0, pl.ds(0, PER_KIND)], r_near.at[t, k, 0])
        below = states.at[t, (y + 3) % NY, pl.ds(k * PER_KIND, half)]
        send(below, below, s_fw.at[t], r_far.at[t], at_y(1))
        drain(states.at[t, 0, pl.ds(0, PER_KIND)], r_near.at[t, k, 1])
        above = states.at[t, (y + 1) % NY, pl.ds(k * PER_KIND + half, half)]
        send(above, above, s_fw.at[t], r_far.at[t], at_y(3))

    def forward_all(t):
        for k in range(KINDS):
            forward(t, k)

    def pass_on_all(t):
        for k in range(KINDS):
            pass_on(t, k)

    def forward_part(t, part_of):
        for k in range(part_of * KINDS // 2, (part_of + 1) * KINDS // 2):
            forward(t, k)

    def pass_on_part(t, part_of):
        for k in range(part_of * KINDS // 2, (part_of + 1) * KINDS // 2):
            pass_on(t, k)

    def spread_y(t):
        for k in range(KINDS):
            forward(t, k)
            if k >= 2:
                pass_on(t, k - 2)
        for k in range(max(0, KINDS - 2), KINDS):
            pass_on(t, k)

    @pl.when(sec == 0)
    def _():
        merged[0] = part[...]
        drain(merged.at[1], r_part.at[0])
        begin_batch(0)
        begin_chunk(0)
        drain(merged.at[pl.ds(2, 2)], r_part.at[1])
        begin_batch(1)

    drain(kvrx, r_kv)
    r_i, c_i = iota((128, 128), 0), iota((128, 128), 1)
    collect = ((r_i >> 5) == ((c_i >> 2) & 3)) & (((r_i >> 3) & 3) == (c_i & 3)) & ((r_i & 7) == (c_i >> 4))
    collect = jnp.where(collect, 1.0, 0.0).astype(BF16)
    for t in range(16):
        made = dot(collect, kvrx[:, t].reshape(128, 128)).astype(BF16).reshape(2, 2, 32, 128)
        for h in range(2):
            kvrows[t // 2, (t % 2) * 2 + h] = made[h]

    @pl.when(sec == 0)
    def _():
        send(kvrows.at[:, :, 1 - core], kvall.at[:, :, core], s_kvm, r_kvm, sibling)
        pltpu.make_async_copy(kvrows.at[:, :, core], kvall.at[:, :, core], r_kvm).start()
        forward_part(0, 0)
        begin_chunk(1)
        forward_part(0, 1)
        drain(kvall.at[:, :, pl.ds(0, 2)], r_kvm)

        @pl.loop(0, NZ)
        def _(zz):
            for yy in range(NY):
                mine = kvall[zz, yy, 0:2].reshape(64, 128)
                made = dot_t(gain_of(zz * NY + yy), mine)
                made = jnp.concatenate([made, jnp.zeros((128, 192), F32)], axis=1)
                weights[zz, yy, :, 256:512] = made.astype(BF16)

    @pl.when(sec > 0)
    def _():
        slot = 2 * y + core
        for i, dy in enumerate((1, 3)):
            for other in (core, 1 - core):
                to = (sec, z * NY + (y + dy) % NY, other)
                send(kvrows.at[:, :, other], kvall.at[:, :, slot], s_kvm, r_kvn.at[i], to)
        send(kvrows.at[:, :, 1 - core], kvall.at[:, :, slot], s_kvm, r_kvm, sibling)
        pltpu.make_async_copy(kvrows.at[:, :, core], kvall.at[:, :, slot], r_kvm).start()
        drain(kvall.at[:, :, pl.ds(0, 2)], r_kvn.at[0])
        below = kvall.at[:, :, 2 * ((y + 3) % NY) + 1]
        send(below, below, s_kvm, r_kvf, at_y(1))
        drain(kvall.at[:, :, pl.ds(0, 2)], r_kvn.at[1])
        above = kvall.at[:, :, 2 * ((y + 1) % NY)]
        send(above, above, s_kvm, r_kvf, at_y(3))
        drain(kvall.at[:, :, pl.ds(0, 2)], r_kvm)
        drain(kvall.at[:, :, pl.ds(0, 2)], r_kvf)

        def prepare(low, high):
            @pl.loop(low, high)
            def _(zz):
                for yy in range(NY):
                    made = dot_t(gain_of(zz * NY + yy), kvall[zz, yy].reshape(256, 128)).astype(BF16)
                    weights[zz, yy, :, 256:512] = dot(made, order[...]).astype(BF16)

        prepare(0, NZ // 2)

        @pl.when(sec == 1)
        def _():
            forward_part(0, 0)

        prepare(NZ // 2, NZ)

        @pl.when(sec == 1)
        def _():
            forward_part(0, 1)
            pass_on_all(0)

        @pl.when(sec > 1)
        def _():
            spread_y(0)

    def project(t, meanwhile=lambda: None):
        def products(ya, yb):
            def step(slot, carry):
                acc, squares = carry
                zz = (z + 2 * NZ + 1 - slot) % NZ
                x = jnp.concatenate([states[t, ya, slot], states[t, yb, slot]], axis=1)
                w = jnp.concatenate([weights[zz, ya], weights[zz, yb]], axis=0)
                acc = acc + dot(x, w)
                xf = x.astype(F32)
                for piece in (xf[:, 0:128], xf[:, 128:256]):
                    squares = squares + piece * piece
                return acc, squares

            return step

        sums = jnp.zeros((tc, 512), F32), jnp.zeros((tc, 128), F32)
        sums = lax.fori_loop(0, NZ, products(y, (y + 1) % NY), sums, unroll=4)
        drain(states.at[t, 0], r_far.at[t])
        acc, squares = lax.fori_loop(0, NZ, products((y + 2) % NY, (y + 3) % NY), sums, unroll=4)
        total = jnp.broadcast_to(jnp.sum(squares, axis=1, keepdims=True), (tc, 128))
        own_q, own_kv = acc[:, 0:128], acc[:, 256:512]
        xs[t, :, 0:128] = acc[:, 128:256]
        xs[t, :, 128:384] = own_kv
        xs[t, :, 384:512] = total
        send(xs.at[t], xr.at[t], s_x.at[t], r_x.at[t], sibling)
        meanwhile()
        drain(xr.at[t], r_x.at[t])
        scale = lax.rsqrt((total + xr[t, :, 384:512]) * (1.0 / 8192.0) + 1e-6)
        scales = jnp.concatenate([scale, scale], axis=1)
        kv = ((own_kv + xr[t, :, 128:384]) * scales).astype(BF16)
        queries[t] = ((own_q + xr[t, :, 0:128]) * scale).astype(BF16)
        return kv

    def attend(t):
        here = slice(t * tc, (t + 1) * tc)
        first = (t * tc // batch) * batch
        span = (t + 1) * tc - first
        pos, begin, _, _ = place(tc, t * tc)
        column = first + iota((tc, span), 1)
        allowed = (column >= begin) & (column <= pos)
        scores = dot_t(queries[t], keys[first : first + span, :]) * (1.0 / math.sqrt(HD))
        scores = jnp.where(allowed, scores, -1e30)
        weight = jnp.exp(scores - jnp.max(scores, axis=1, keepdims=True))
        probs = (weight / jnp.sum(weight, axis=1, keepdims=True)).astype(BF16)
        attended = dot(probs, values[first : first + span, :])
        state = states[t, y, slot_of(0)].astype(F32) + attended
        out_ref[here, :] = state.astype(BF16)

        @pl.when(sec < depth - 1)
        def _():
            for dz in SENDS:
                send(
                    out_ref.at[pl.ds(t * tc, tc)],
                    states.at[t, y, slot_of(dz)],
                    s_st.at[t],
                    r_st.at[t, slot_of(dz) // PER_KIND],
                    at_z(dz, sec + 1),
                )

    def attend_shared(t):
        here = slice(t * tc, (t + 1) * tc)
        drain(kvx.at[t, pl.ds(0, 3)], r_kx.at[t])
        kv = dot(jnp.concatenate([kvx[t, yy] for yy in range(NY)], axis=1), spread[...]).astype(BF16)
        keys[here, :] = kv[:, 0:128]
        values[here, :] = kv[:, 128:256]
        attend(t)

    @pl.when(sec == 0)
    def _():
        def first_half(t):
            if t < CHUNKS:
                forward_part(t, 0)
            if t + 1 < CHUNKS:
                begin_chunk(t + 1)

        def second_half(t):
            if t < CHUNKS:
                forward_part(t, 1)

        pass_on_all(0)
        first_half(1)
        second_half(1)
        for t in range(CHUNKS):
            kv = project(t)
            kvx[t, y] = kv[:, 0:128]
            for dy in (2, 1, 3):
                send(kvx.at[t, y], kvx.at[t, y], s_kx.at[t], r_kx.at[t], at_y(dy))
            if t + 1 < CHUNKS:
                pass_on_all(t + 1)
            first_half(t + 2)
            attend_shared(t)
            second_half(t + 2)

    @pl.when(sec > 0)
    def _():
        for t in range(CHUNKS):
            here = slice(t * tc, (t + 1) * tc)
            if t > 0:
                pass_on_part(t, 1)
            if t + 1 < CHUNKS:
                forward_all(t + 1)

            def early():
                if t + 1 < CHUNKS:
                    pass_on_part(t + 1, 0)

            kv = project(t, early)
            keys[here, :] = kv[:, 0:128]
            values[here, :] = kv[:, 128:256]
            attend(t)

    drain(rows.at[core, pl.ds(0, 7), 0], s_act.at[0])
    drain(rows.at[core, :, pl.ds(0, 3)], s_act.at[1])
    drain(rows.at[core], s_act.at[2])
    drain(wq_sib, s_wq)
    drain(kvrx.at[pl.ds(0, 7)], s_kv)

    @pl.when(sec == 0)
    def _():
        drain(kvall.at[:, :, 0], s_kvm)

    @pl.when(sec > 0)
    def _():
        drain(part, s_part)
        drain(kvall.at[:, :, pl.ds(0, 7)], s_kvm)

    for t in range(CHUNKS):

        @pl.when(sec == 0)
        def _():
            drain(states.at[t, 0, pl.ds(0, 7)], s_init.at[t])
            drain(kvx.at[t, pl.ds(0, 3)], s_kx.at[t])

        @pl.when(sec < depth - 1)
        def _():
            drain(states.at[t, 0], s_st.at[t])

        drain(states.at[t, pl.ds(0, 3)], s_fw.at[t])
        drain(xs.at[t], s_x.at[t])


def shards(text_embed, patch, mw, bias, gain, wq, wk, wv, images, texts):
    tokens = text_embed.shape[0]
    tc = tokens // CHUNKS
    vmem = pl.BlockSpec(memory_space=pltpu.VMEM)
    smem = pl.BlockSpec(memory_space=pltpu.SMEM)
    hbm = pl.BlockSpec(memory_space=pl.ANY)
    dma = pltpu.SemaphoreType.DMA
    scratch = [
        pltpu.VMEM((64, 128), F32),
        pltpu.VMEM((40, 128), F32),
        pltpu.VMEM((40, 128), BF16),
        pltpu.VMEM((2, NZ, NY, 40, 128), BF16),
        pltpu.VMEM((2560, 128), F32),
        pltpu.VMEM((64, 128), BF16),
        pltpu.VMEM((4, 64, 128), BF16),
        pltpu.VMEM((tokens, 128), BF16),
        pltpu.VMEM((NZ, 16, 16, 128), BF16),
        pltpu.VMEM((NZ, 16, 16, 128), BF16),
        pltpu.VMEM((NZ, NY, 2, 32, 128), BF16),
        pltpu.VMEM((NZ, NY, 8, 32, 128), BF16),
        pltpu.VMEM((NZ, NY, 2, 128, 128), BF16),
        pltpu.VMEM((NZ, NY, 128, 128), BF16),
        pltpu.VMEM(mw.shape, BF16),
        pltpu.VMEM((NZ, NY, 128, 512), BF16),
        pltpu.VMEM((CHUNKS, NY, NZ, tc, 128), BF16),
        pltpu.VMEM((CHUNKS, tc, 512), F32),
        pltpu.VMEM((CHUNKS, tc, 512), F32),
        pltpu.VMEM((CHUNKS, NY, tc, 128), BF16),
        pltpu.VMEM((512, 256), BF16),
        pltpu.VMEM((256, 256), BF16),
        pltpu.VMEM((CHUNKS, tc, 128), BF16),
        pltpu.VMEM((tokens, 128), BF16),
        pltpu.VMEM((tokens, 128), BF16),
        dma,
        dma,
        dma((3,)),
        dma,
        dma,
        dma,
        dma,
        dma,
        dma,
        dma,
        dma,
        dma,
        dma((2,)),
        dma,
        dma,
        dma((2,)),
        dma((CHUNKS,)),
        dma((CHUNKS,)),
        dma((CHUNKS, KINDS)),
        dma((CHUNKS,)),
        dma((CHUNKS, KINDS, 2)),
        dma((CHUNKS,)),
        dma((CHUNKS,)),
        dma((CHUNKS,)),
        dma((CHUNKS,)),
        dma((CHUNKS,)),
    ]
    out = pl.pallas_call(
        kernel,
        out_shape=jax.ShapeDtypeStruct((tokens, 128), BF16),
        in_specs=[smem, smem, vmem, vmem, hbm, vmem, vmem, hbm, vmem, vmem],
        out_specs=vmem,
        scratch_shapes=scratch,
        compiler_params=pltpu.CompilerParams(
            collective_id=0, has_side_effects=True, vmem_limit_bytes=60 * 1024 * 1024
        ),
        name="prefill",
    )(
        images,
        texts,
        text_embed,
        patch,
        mw,
        bias.reshape(1, 128),
        gain,
        wq.reshape(NZ, NY, 2, 128, 128),
        jnp.swapaxes(wk[0], 0, 1),
        jnp.swapaxes(wv[0], 0, 1),
    )
    return out[None]


def solution(mesh):
    in_specs = (
        P(None, ("seq", "mp")),
        P(("section", "seq", "mp"), None),
        P(None, ("seq", "mp")),
        P(("seq", "mp")),
        P("section", None),
        P("section", None, ("seq", "mp")),
        P("section", None, ("seq", "mp")),
        P("section", None, ("seq", "mp")),
        P(),
        P(),
    )
    out_specs = P("section", None, ("seq", "mp"))
    return jax.shard_map(shards, mesh=mesh, in_specs=in_specs, out_specs=out_specs, check_vma=False)
```

```python
import functools
import math

import jax
import jax.numpy as jnp
from jax import lax
from jax.experimental import pallas as pl
from jax.experimental.pallas import tpu as pltpu
from jax.sharding import PartitionSpec as P

MESH = pl.DeviceIdType.MESH
F32 = jnp.float32
BF16 = jnp.bfloat16
HD = 128
NY = 4
NZ = 8
CHUNKS = 4
Z_ORDER = (4, 3, 5, 2, 6, 1, 7)
KINDS = 4
PER_KIND = NZ // KINDS
VISIT = (0, 1, 3, 2)
SENDS = (0, 7, 1, 2, 6, 5, 3, 4)


def iota(shape, dim):
    return lax.broadcasted_iota(jnp.int32, shape, dim)


def dot(a, b):
    return lax.dot_general(a, b, (((1,), (0,)), ((), ())), preferred_element_type=F32)


def dot_t(a, b):
    return lax.dot_general(a, b, (((1,), (1,)), ((), ())), preferred_element_type=F32)


def drain(ref, sem):
    pltpu.make_async_copy(ref, ref, sem).wait()


def kernel(
    images_ref,
    texts_ref,
    text_ref,
    patch_ref,
    mw_ref,
    bias_ref,
    gain_ref,
    wq_ref,
    wk_ref,
    wv_ref,
    out_ref,
    gains,
    actf,
    act,
    rows,
    rowsf,
    part,
    merged,
    start,
    kvtx,
    kvrx,
    kvrows,
    kvall,
    wq_own,
    wq_sib,
    mw_here,
    weights,
    states,
    xs,
    xr,
    kvx,
    spread,
    order,
    queries,
    keys,
    values,
    l_wq,
    l_mw,
    s_act,
    r_act1,
    r_act2,
    r_act3,
    s_wq,
    r_wq,
    s_kv,
    r_kv,
    s_kvm,
    r_kvm,
    r_kvn,
    r_kvf,
    s_part,
    r_part,
    s_init,
    s_st,
    r_st,
    s_fw,
    r_near,
    r_far,
    s_x,
    r_x,
    s_kx,
    r_kx,
):
    sec = lax.axis_index("section")
    seq = lax.axis_index("seq")
    core = lax.axis_index("mp")
    depth = lax.axis_size("section")
    z = seq // NY
    y = seq % NY
    tokens = out_ref.shape[0]
    tc = tokens // CHUNKS
    batch = tokens // images_ref.shape[0]

    def at_z(dz, s=None):
        return (sec if s is None else s, ((z + dz) % NZ) * NY + y, core)

    def at_y(dy):
        return (sec, z * NY + (y + dy) % NY, core)

    sibling = (sec, seq, 1 - core)

    def send(src, dst, ssem, rsem, device):
        pltpu.make_async_remote_copy(
            src_ref=src, dst_ref=dst, send_sem=ssem, recv_sem=rsem, device_id=device, device_id_type=MESH
        ).start()

    barrier = pltpu.get_barrier_semaphore()

    def greet(device):
        pl.semaphore_signal(barrier, inc=1, device_id=device, device_id_type=MESH)

    for dz in Z_ORDER:
        greet(at_z(dz))
    for dy in (2, 1, 3):
        greet(at_y(dy))
    greet(sibling)

    @pl.when(sec > 0)
    def _():
        for dz in (0,) + Z_ORDER:
            greet(at_z(dz, sec - 1))
        for dy in (1, 3):
            greet((sec, z * NY + (y + dy) % NY, 1 - core))

    @pl.when(sec == 0)
    def _():
        for other in (1, 2, 3):
            greet((other, seq, core))

    load_wq = pltpu.make_async_copy(wq_ref, wq_own, l_wq)
    load_wq.start()
    load_mw = pltpu.make_async_copy(mw_ref, mw_here, l_mw)
    load_mw.start()
    for k in range(40):
        actf[k : k + 1, :] = patch_ref[:, k * 128 : (k + 1) * 128].astype(F32)
    xa = actf[...]
    act[...] = (0.5 * xa * (1.0 + lax.erf(xa * math.sqrt(0.5)))).astype(BF16)
    for k in range(64):
        gains[k : k + 1, :] = gain_ref[:, k * 128 : (k + 1) * 128].astype(F32)

    r_i, c_i = iota((128, 128), 0), iota((128, 128), 1)
    deal = (
        ((r_i >> 4) == (c_i & 7)) & (((r_i >> 2) & 3) == (c_i >> 5)) & ((r_i & 3) == ((c_i >> 3) & 3))
    )
    deal = jnp.where(deal, 1.0, 0.0).astype(BF16)
    for t in range(16):
        pieces = []
        for b in range(4):
            lanes = slice((4 * t + b) * 128, (4 * t + b + 1) * 128)
            pieces += [wk_ref[:, lanes], wv_ref[:, lanes]]
        kvtx[:, t] = dot(deal, jnp.concatenate(pieces, axis=0)).astype(BF16).reshape(NZ, 16, 128)
    r_i, c_i = iota((512, 256), 0), iota((512, 256), 1)
    lane = r_i & 127
    feature = 2 * ((lane & 7) * 8 + (r_i >> 7) * 2 + ((lane >> 5) & 1)) + ((lane >> 3) & 1)
    natural = (lane < 64) & (c_i == ((lane >> 4) & 1) * 128 + feature)
    spread[...] = jnp.where(natural, 1.0, 0.0).astype(BF16)
    r_i, c_i = iota((256, 256), 0), iota((256, 256), 1)
    feature = 2 * ((r_i & 7) * 8 + (r_i >> 5)) + ((r_i >> 3) & 1)
    order[...] = jnp.where(c_i == ((r_i >> 4) & 1) * 128 + feature, 1.0, 0.0).astype(BF16)

    def gain_of(q):
        g = gains[pl.ds(2 * q + core, 1), :]
        return jnp.where(iota((128, 128), 0) == iota((128, 128), 1), g, 0.0).astype(BF16)

    load_wq.wait()

    @pl.loop(0, NZ)
    def _(zz):
        for yy in range(NY):
            weights[zz, yy, :, 0:128] = dot(gain_of(zz * NY + yy), wq_own[zz, yy, core]).astype(BF16)

    @pl.when(sec == 0)
    def _():
        pl.semaphore_wait(barrier, 19)

    @pl.when((sec > 0) & (sec < depth - 1))
    def _():
        pl.semaphore_wait(barrier, 22)

    @pl.when(sec == depth - 1)
    def _():
        pl.semaphore_wait(barrier, 14)

    for dz in (1, 7, 2, 6, 3, 5, 4):
        slot = (dz + 1) % NZ
        send(act, rows.at[core, y, slot], s_act.at[0], r_act1.at[slot // 4], at_z(dz))
    pltpu.make_async_copy(act, rows.at[core, y, 1], r_act1.at[0]).start()

    def deal_rows():
        for dz in Z_ORDER:
            send(kvtx.at[(z + dz) % NZ], kvrx.at[z], s_kv, r_kv, at_z(dz))
        pltpu.make_async_copy(kvtx.at[z], kvrx.at[z], r_kv).start()


    @pl.when(sec == 0)
    def _():
        deal_rows()

    send(wq_own.at[:, :, 1 - core], wq_sib, s_wq, r_wq, sibling)

    for k in range(2):
        drain(rows.at[core, 0, pl.ds(0, 4)], r_act1.at[k])
        block = rows.at[core, y, pl.ds(4 * k, 4)]
        for dy in (2, 1, 3):
            send(block, block, s_act.at[1], r_act2, at_y(dy))

    @pl.when(sec > 0)
    def _():
        deal_rows()

    drain(wq_sib, r_wq)

    @pl.loop(0, NZ)
    def _(zz):
        for yy in range(NY):
            weights[zz, yy, :, 128:256] = dot(gain_of(zz * NY + yy), wq_sib[zz, yy]).astype(BF16)

    drain(rows.at[core, pl.ds(0, 3)], r_act2)
    send(rows.at[core], rows.at[core], s_act.at[2], r_act3, sibling)
    drain(rows.at[core], r_act3)

    for p in range(2):
        for yy in range(NY):
            for zz in range(NZ):
                at = ((p * NY + yy) * NZ + zz) * 40
                rowsf[at : at + 40, :] = rows[p, yy, zz].astype(F32)
    load_mw.wait()
    acc = jnp.broadcast_to(bias_ref[...].astype(F32), (64, 128))
    for k in range(20):
        xk = jnp.concatenate(
            [rowsf[pl.ds(2 * k, 64, stride=40), :], rowsf[pl.ds(2 * k + 1, 64, stride=40), :]], axis=1
        ).astype(BF16)
        acc = acc + dot(xk, mw_here[256 * k : 256 * (k + 1), :])
    part[...] = acc.astype(BF16)

    @pl.when(sec == 1)
    def _():
        send(part, merged.at[1], s_part, r_part.at[0], (0, seq, core))

    @pl.when(sec > 1)
    def _():
        send(part, merged.at[sec], s_part, r_part.at[1], (0, seq, core))

    def place(rows_here, first):
        pos = first + iota((rows_here, 1), 0)
        begin = jnp.zeros((rows_here, 1), jnp.int32)
        count = jnp.zeros((rows_here, 1), jnp.int32)
        earlier = jnp.zeros((rows_here, 1), jnp.int32)
        at, seen = jnp.int32(0), jnp.int32(0)
        for b in range(images_ref.shape[0]):
            for r in range(images_ref.shape[1]):
                image, text = images_ref[b, r], texts_ref[b, r]
                inside = pos >= at
                begin = jnp.where(inside, at, begin)
                count = jnp.where(inside, image, count)
                earlier = jnp.where(inside, seen, earlier)
                at, seen = at + image + text, seen + image
        return pos, begin, count, earlier

    def begin_batch(m):
        first, count_here = m * batch, batch
        pos, begin, count, earlier = place(count_here, first)
        offset = pos - begin
        is_image = (offset >= 1) & (offset <= count)
        row = earlier + offset - 1 - m * 128
        away = (z + NZ + 1 - ((row & 63) >> 3)) & (NZ - 1)
        slot = (row & 64) + ((row & 1) << 5) + (((row >> 1) & 3) << 3) + away
        chosen = (iota((count_here, 128), 1) == slot) & is_image
        picked = dot(
            jnp.where(chosen, 1.0, 0.0).astype(BF16), merged[2 * m : 2 * m + 2].reshape(128, 128)
        )
        text = text_ref[first : first + batch, :].astype(F32)
        start[first : first + batch, :] = jnp.where(is_image, picked, text).astype(BF16)

    def slot_of(dz):
        return (dz + 1) % NZ

    def begin_chunk(t):
        src = start.at[pl.ds(t * tc, tc)]
        for dz in SENDS:
            if dz:
                send(src, states.at[t, y, slot_of(dz)], s_init.at[t], r_st.at[t, slot_of(dz) // PER_KIND], at_z(dz))
        pltpu.make_async_copy(src, states.at[t, y, slot_of(0)], r_st.at[t, slot_of(0) // PER_KIND]).start()

    def forward(t, i):
        k = VISIT[i]
        drain(states.at[t, 0, pl.ds(0, PER_KIND)], r_st.at[t, k])
        block = states.at[t, y, pl.ds(k * PER_KIND, PER_KIND)]
        send(block, block, s_fw.at[t], r_near.at[t, k, 0], at_y(1))
        send(block, block, s_fw.at[t], r_near.at[t, k, 1], at_y(3))

    def pass_on(t, i):
        k, half = VISIT[i], PER_KIND // 2
        drain(states.at[t, 0, pl.ds(0, PER_KIND)], r_near.at[t, k, 0])
        below = states.at[t, (y + 3) % NY, pl.ds(k * PER_KIND, half)]
        send(below, below, s_fw.at[t], r_far.at[t], at_y(1))
        drain(states.at[t, 0, pl.ds(0, PER_KIND)], r_near.at[t, k, 1])
        above = states.at[t, (y + 1) % NY, pl.ds(k * PER_KIND + half, half)]
        send(above, above, s_fw.at[t], r_far.at[t], at_y(3))

    def forward_all(t):
        for k in range(KINDS):
            forward(t, k)

    def pass_on_all(t):
        for k in range(KINDS):
            pass_on(t, k)

    def forward_part(t, part_of):
        for k in range(part_of * KINDS // 2, (part_of + 1) * KINDS // 2):
            forward(t, k)

    def pass_on_part(t, part_of):
        for k in range(part_of * KINDS // 2, (part_of + 1) * KINDS // 2):
            pass_on(t, k)

    def spread_y(t):
        for k in range(KINDS):
            forward(t, k)
            if k >= 2:
                pass_on(t, k - 2)
        for k in range(max(0, KINDS - 2), KINDS):
            pass_on(t, k)

    @pl.when(sec == 0)
    def _():
        merged[0] = part[...]
        drain(merged.at[1], r_part.at[0])
        begin_batch(0)
        begin_chunk(0)
        drain(merged.at[pl.ds(2, 2)], r_part.at[1])
        begin_batch(1)

    drain(kvrx, r_kv)
    r_i, c_i = iota((128, 128), 0), iota((128, 128), 1)
    collect = ((r_i >> 5) == ((c_i >> 2) & 3)) & (((r_i >> 3) & 3) == (c_i & 3)) & ((r_i & 7) == (c_i >> 4))
    collect = jnp.where(collect, 1.0, 0.0).astype(BF16)
    for t in range(16):
        made = dot(collect, kvrx[:, t].reshape(128, 128)).astype(BF16).reshape(2, 2, 32, 128)
        for h in range(2):
            kvrows[t // 2, (t % 2) * 2 + h] = made[h]

    @pl.when(sec == 0)
    def _():
        send(kvrows.at[:, :, 1 - core], kvall.at[:, :, core], s_kvm, r_kvm, sibling)
        pltpu.make_async_copy(kvrows.at[:, :, core], kvall.at[:, :, core], r_kvm).start()
        forward_part(0, 0)
        begin_chunk(1)
        forward_part(0, 1)
        drain(kvall.at[:, :, pl.ds(0, 2)], r_kvm)

        @pl.loop(0, NZ)
        def _(zz):
            for yy in range(NY):
                mine = kvall[zz, yy, 0:2].reshape(64, 128)
                made = dot_t(gain_of(zz * NY + yy), mine)
                made = jnp.concatenate([made, jnp.zeros((128, 192), F32)], axis=1)
                weights[zz, yy, :, 256:512] = made.astype(BF16)

    @pl.when(sec > 0)
    def _():
        slot = 2 * y + core
        for i, dy in enumerate((1, 3)):
            for other in (core, 1 - core):
                to = (sec, z * NY + (y + dy) % NY, other)
                send(kvrows.at[:, :, other], kvall.at[:, :, slot], s_kvm, r_kvn.at[i], to)
        send(kvrows.at[:, :, 1 - core], kvall.at[:, :, slot], s_kvm, r_kvm, sibling)
        pltpu.make_async_copy(kvrows.at[:, :, core], kvall.at[:, :, slot], r_kvm).start()
        drain(kvall.at[:, :, pl.ds(0, 2)], r_kvn.at[0])
        below = kvall.at[:, :, 2 * ((y + 3) % NY) + 1]
        send(below, below, s_kvm, r_kvf, at_y(1))
        drain(kvall.at[:, :, pl.ds(0, 2)], r_kvn.at[1])
        above = kvall.at[:, :, 2 * ((y + 1) % NY)]
        send(above, above, s_kvm, r_kvf, at_y(3))
        drain(kvall.at[:, :, pl.ds(0, 2)], r_kvm)
        drain(kvall.at[:, :, pl.ds(0, 2)], r_kvf)

        def prepare(low, high):
            @pl.loop(low, high)
            def _(zz):
                for yy in range(NY):
                    made = dot_t(gain_of(zz * NY + yy), kvall[zz, yy].reshape(256, 128)).astype(BF16)
                    weights[zz, yy, :, 256:512] = dot(made, order[...]).astype(BF16)

        prepare(0, NZ // 2)

        @pl.when(sec == 1)
        def _():
            forward_part(0, 0)

        prepare(NZ // 2, NZ)

        @pl.when(sec == 1)
        def _():
            forward_part(0, 1)
            pass_on_all(0)

        @pl.when(sec > 1)
        def _():
            spread_y(0)

    def project(t, meanwhile=lambda: None):
        def products(ya, yb):
            def step(slot, carry):
                acc, squares = carry
                zz = (z + 2 * NZ + 1 - slot) % NZ
                x = jnp.concatenate([states[t, ya, slot], states[t, yb, slot]], axis=1)
                w = jnp.concatenate([weights[zz, ya], weights[zz, yb]], axis=0)
                acc = acc + dot(x, w)
                xf = x.astype(F32)
                for piece in (xf[:, 0:128], xf[:, 128:256]):
                    squares = squares + piece * piece
                return acc, squares

            return step

        sums = jnp.zeros((tc, 512), F32), jnp.zeros((tc, 128), F32)
        sums = lax.fori_loop(0, NZ, products(y, (y + 1) % NY), sums, unroll=4)
        drain(states.at[t, 0], r_far.at[t])
        acc, squares = lax.fori_loop(0, NZ, products((y + 2) % NY, (y + 3) % NY), sums, unroll=4)
        total = jnp.broadcast_to(jnp.sum(squares, axis=1, keepdims=True), (tc, 128))
        own_q, own_kv = acc[:, 0:128], acc[:, 256:512]
        xs[t, :, 0:128] = acc[:, 128:256]
        xs[t, :, 128:384] = own_kv
        xs[t, :, 384:512] = total
        send(xs.at[t], xr.at[t], s_x.at[t], r_x.at[t], sibling)
        meanwhile()
        drain(xr.at[t], r_x.at[t])
        scale = lax.rsqrt((total + xr[t, :, 384:512]) * (1.0 / 8192.0) + 1e-6)
        scales = jnp.concatenate([scale, scale], axis=1)
        kv = ((own_kv + xr[t, :, 128:384]) * scales).astype(BF16)
        queries[t] = ((own_q + xr[t, :, 0:128]) * scale).astype(BF16)
        return kv

    def attend(t):
        here = slice(t * tc, (t + 1) * tc)
        first = (t * tc // batch) * batch
        span = (t + 1) * tc - first
        pos, begin, _, _ = place(tc, t * tc)
        column = first + iota((tc, span), 1)
        allowed = (column >= begin) & (column <= pos)
        scores = dot_t(queries[t], keys[first : first + span, :]) * (1.0 / math.sqrt(HD))
        scores = jnp.where(allowed, scores, -1e30)
        weight = jnp.exp(scores - jnp.max(scores, axis=1, keepdims=True))
        probs = (weight / jnp.sum(weight, axis=1, keepdims=True)).astype(BF16)
        attended = dot(probs, values[first : first + span, :])
        state = states[t, y, slot_of(0)].astype(F32) + attended
        out_ref[here, :] = state.astype(BF16)

        @pl.when(sec < depth - 1)
        def _():
            for dz in SENDS:
                send(
                    out_ref.at[pl.ds(t * tc, tc)],
                    states.at[t, y, slot_of(dz)],
                    s_st.at[t],
                    r_st.at[t, slot_of(dz) // PER_KIND],
                    at_z(dz, sec + 1),
                )

    def attend_shared(t):
        here = slice(t * tc, (t + 1) * tc)
        drain(kvx.at[t, pl.ds(0, 3)], r_kx.at[t])
        kv = dot(jnp.concatenate([kvx[t, yy] for yy in range(NY)], axis=1), spread[...]).astype(BF16)
        keys[here, :] = kv[:, 0:128]
        values[here, :] = kv[:, 128:256]
        attend(t)

    @pl.when(sec == 0)
    def _():
        def first_half(t):
            if t < CHUNKS:
                forward_part(t, 0)
            if t + 1 < CHUNKS:
                begin_chunk(t + 1)

        def second_half(t):
            if t < CHUNKS:
                forward_part(t, 1)

        pass_on_all(0)
        first_half(1)
        second_half(1)
        for t in range(CHUNKS):
            kv = project(t)
            kvx[t, y] = kv[:, 0:128]
            for dy in (2, 1, 3):
                send(kvx.at[t, y], kvx.at[t, y], s_kx.at[t], r_kx.at[t], at_y(dy))
            if t + 1 < CHUNKS:
                pass_on_all(t + 1)
            first_half(t + 2)
            attend_shared(t)
            second_half(t + 2)

    @pl.when(sec > 0)
    def _():
        for t in range(CHUNKS):
            here = slice(t * tc, (t + 1) * tc)
            if t > 0:
                pass_on_part(t, 1)
            if t + 1 < CHUNKS:
                forward_all(t + 1)

            def early():
                if t + 1 < CHUNKS:
                    pass_on_part(t + 1, 0)

            kv = project(t, early)
            keys[here, :] = kv[:, 0:128]
            values[here, :] = kv[:, 128:256]
            attend(t)

    drain(rows.at[core, 0, pl.ds(0, 7)], s_act.at[0])
    drain(rows.at[core, pl.ds(0, 3)], s_act.at[1])
    drain(rows.at[core], s_act.at[2])
    drain(wq_sib, s_wq)
    drain(kvrx.at[pl.ds(0, 7)], s_kv)

    @pl.when(sec == 0)
    def _():
        drain(kvall.at[:, :, 0], s_kvm)

    @pl.when(sec > 0)
    def _():
        drain(part, s_part)
        drain(kvall.at[:, :, pl.ds(0, 7)], s_kvm)

    for t in range(CHUNKS):

        @pl.when(sec == 0)
        def _():
            drain(states.at[t, 0, pl.ds(0, 7)], s_init.at[t])
            drain(kvx.at[t, pl.ds(0, 3)], s_kx.at[t])

        @pl.when(sec < depth - 1)
        def _():
            drain(states.at[t, 0], s_st.at[t])

        drain(states.at[t, pl.ds(0, 3)], s_fw.at[t])
        drain(xs.at[t], s_x.at[t])


def shards(text_embed, patch, mw, bias, gain, wq, wk, wv, images, texts):
    tokens = text_embed.shape[0]
    tc = tokens // CHUNKS
    vmem = pl.BlockSpec(memory_space=pltpu.VMEM)
    smem = pl.BlockSpec(memory_space=pltpu.SMEM)
    hbm = pl.BlockSpec(memory_space=pl.ANY)
    dma = pltpu.SemaphoreType.DMA
    scratch = [
        pltpu.VMEM((64, 128), F32),
        pltpu.VMEM((40, 128), F32),
        pltpu.VMEM((40, 128), BF16),
        pltpu.VMEM((2, NY, NZ, 40, 128), BF16),
        pltpu.VMEM((2560, 128), F32),
        pltpu.VMEM((64, 128), BF16),
        pltpu.VMEM((4, 64, 128), BF16),
        pltpu.VMEM((tokens, 128), BF16),
        pltpu.VMEM((NZ, 16, 16, 128), BF16),
        pltpu.VMEM((NZ, 16, 16, 128), BF16),
        pltpu.VMEM((NZ, NY, 2, 32, 128), BF16),
        pltpu.VMEM((NZ, NY, 8, 32, 128), BF16),
        pltpu.VMEM((NZ, NY, 2, 128, 128), BF16),
        pltpu.VMEM((NZ, NY, 128, 128), BF16),
        pltpu.VMEM(mw.shape, BF16),
        pltpu.VMEM((NZ, NY, 128, 512), BF16),
        pltpu.VMEM((CHUNKS, NY, NZ, tc, 128), BF16),
        pltpu.VMEM((CHUNKS, tc, 512), F32),
        pltpu.VMEM((CHUNKS, tc, 512), F32),
        pltpu.VMEM((CHUNKS, NY, tc, 128), BF16),
        pltpu.VMEM((512, 256), BF16),
        pltpu.VMEM((256, 256), BF16),
        pltpu.VMEM((CHUNKS, tc, 128), BF16),
        pltpu.VMEM((tokens, 128), BF16),
        pltpu.VMEM((tokens, 128), BF16),
        dma,
        dma,
        dma((3,)),
        dma((2,)),
        dma,
        dma,
        dma,
        dma,
        dma,
        dma,
        dma,
        dma,
        dma((2,)),
        dma,
        dma,
        dma((2,)),
        dma((CHUNKS,)),
        dma((CHUNKS,)),
        dma((CHUNKS, KINDS)),
        dma((CHUNKS,)),
        dma((CHUNKS, KINDS, 2)),
        dma((CHUNKS,)),
        dma((CHUNKS,)),
        dma((CHUNKS,)),
        dma((CHUNKS,)),
        dma((CHUNKS,)),
    ]
    out = pl.pallas_call(
        kernel,
        out_shape=jax.ShapeDtypeStruct((tokens, 128), BF16),
        in_specs=[smem, smem, vmem, vmem, hbm, vmem, vmem, hbm, vmem, vmem],
        out_specs=vmem,
        scratch_shapes=scratch,
        compiler_params=pltpu.CompilerParams(
            collective_id=0, has_side_effects=True, vmem_limit_bytes=60 * 1024 * 1024
        ),
        name="prefill",
    )(
        images,
        texts,
        text_embed,
        patch,
        mw,
        bias.reshape(1, 128),
        gain,
        wq.reshape(NZ, NY, 2, 128, 128),
        jnp.swapaxes(wk[0], 0, 1),
        jnp.swapaxes(wv[0], 0, 1),
    )
    return out[None]


def solution(mesh):
    in_specs = (
        P(None, ("seq", "mp")),
        P(("section", "seq", "mp"), None),
        P(None, ("seq", "mp")),
        P(("seq", "mp")),
        P("section", None),
        P("section", None, ("seq", "mp")),
        P("section", None, ("seq", "mp")),
        P("section", None, ("seq", "mp")),
        P(),
        P(),
    )
    out_specs = P("section", None, ("seq", "mp"))
    return jax.shard_map(shards, mesh=mesh, in_specs=in_specs, out_specs=out_specs, check_vma=False)
```

```python
import functools
import math

import jax
import jax.numpy as jnp
from jax import lax
from jax.experimental import pallas as pl
from jax.experimental.pallas import tpu as pltpu
from jax.sharding import PartitionSpec as P

MESH = pl.DeviceIdType.MESH
F32 = jnp.float32
BF16 = jnp.bfloat16
HD = 128
NY = 4
NZ = 8
CHUNKS = 4
Z_ORDER = (4, 3, 5, 2, 6, 1, 7)
KINDS = 4
PER_KIND = NZ // KINDS
VISIT = (0, 1, 3, 2)
SENDS = (0, 7, 1, 2, 6, 5, 3, 4)


def iota(shape, dim):
    return lax.broadcasted_iota(jnp.int32, shape, dim)


def dot(a, b):
    return lax.dot_general(a, b, (((1,), (0,)), ((), ())), preferred_element_type=F32)


def dot_t(a, b):
    return lax.dot_general(a, b, (((1,), (1,)), ((), ())), preferred_element_type=F32)


def drain(ref, sem):
    pltpu.make_async_copy(ref, ref, sem).wait()


def kernel(
    images_ref,
    texts_ref,
    text_ref,
    patch_ref,
    mw_ref,
    bias_ref,
    gain_ref,
    wq_ref,
    wk_ref,
    wv_ref,
    out_ref,
    gains,
    actf,
    act,
    rows,
    rowsf,
    part,
    merged,
    start,
    kvtx,
    kvrx,
    kvrows,
    kvall,
    wq_own,
    wq_sib,
    mw_here,
    weights,
    states,
    xs,
    xr,
    kvx,
    spread,
    order,
    queries,
    keys,
    values,
    l_wq,
    l_mw,
    s_act,
    r_act1,
    r_act2,
    r_act3,
    s_wq,
    r_wq,
    s_kv,
    r_kv,
    s_kvm,
    r_kvm,
    r_kvn,
    r_kvf,
    s_part,
    r_part,
    s_init,
    s_st,
    r_st,
    s_fw,
    r_near,
    r_far,
    s_x,
    r_x,
    s_kx,
    r_kx,
):
    sec = lax.axis_index("section")
    seq = lax.axis_index("seq")
    core = lax.axis_index("mp")
    depth = lax.axis_size("section")
    z = seq // NY
    y = seq % NY
    tokens = out_ref.shape[0]
    tc = tokens // CHUNKS
    batch = tokens // images_ref.shape[0]

    def at_z(dz, s=None):
        return (sec if s is None else s, ((z + dz) % NZ) * NY + y, core)

    def at_y(dy):
        return (sec, z * NY + (y + dy) % NY, core)

    sibling = (sec, seq, 1 - core)

    def send(src, dst, ssem, rsem, device):
        pltpu.make_async_remote_copy(
            src_ref=src, dst_ref=dst, send_sem=ssem, recv_sem=rsem, device_id=device, device_id_type=MESH
        ).start()

    barrier = pltpu.get_barrier_semaphore()

    def greet(device):
        pl.semaphore_signal(barrier, inc=1, device_id=device, device_id_type=MESH)

    for dz in Z_ORDER:
        greet(at_z(dz))
    for dy in (2, 1, 3):
        greet(at_y(dy))
    greet(sibling)

    @pl.when(sec > 0)
    def _():
        for dz in (0,) + Z_ORDER:
            greet(at_z(dz, sec - 1))
        for dy in (1, 3):
            greet((sec, z * NY + (y + dy) % NY, 1 - core))

    @pl.when(sec == 0)
    def _():
        for other in (1, 2, 3):
            greet((other, seq, core))

    load_wq = pltpu.make_async_copy(wq_ref, wq_own, l_wq)
    load_wq.start()
    load_mw = pltpu.make_async_copy(mw_ref, mw_here, l_mw)
    load_mw.start()
    for k in range(40):
        actf[k : k + 1, :] = patch_ref[:, k * 128 : (k + 1) * 128].astype(F32)
    xa = actf[...]
    act[...] = (0.5 * xa * (1.0 + lax.erf(xa * math.sqrt(0.5)))).astype(BF16)
    for k in range(64):
        gains[k : k + 1, :] = gain_ref[:, k * 128 : (k + 1) * 128].astype(F32)

    r_i, c_i = iota((128, 128), 0), iota((128, 128), 1)
    deal = (
        ((r_i >> 4) == (c_i & 7)) & (((r_i >> 2) & 3) == (c_i >> 5)) & ((r_i & 3) == ((c_i >> 3) & 3))
    )
    deal = jnp.where(deal, 1.0, 0.0).astype(BF16)
    for t in range(16):
        pieces = []
        for b in range(4):
            lanes = slice((4 * t + b) * 128, (4 * t + b + 1) * 128)
            pieces += [wk_ref[:, lanes], wv_ref[:, lanes]]
        kvtx[:, t] = dot(deal, jnp.concatenate(pieces, axis=0)).astype(BF16).reshape(NZ, 16, 128)
    r_i, c_i = iota((512, 256), 0), iota((512, 256), 1)
    lane = r_i & 127
    feature = 2 * ((lane & 7) * 8 + (r_i >> 7) * 2 + ((lane >> 5) & 1)) + ((lane >> 3) & 1)
    natural = (lane < 64) & (c_i == ((lane >> 4) & 1) * 128 + feature)
    spread[...] = jnp.where(natural, 1.0, 0.0).astype(BF16)
    r_i, c_i = iota((256, 256), 0), iota((256, 256), 1)
    feature = 2 * ((r_i & 7) * 8 + (r_i >> 5)) + ((r_i >> 3) & 1)
    order[...] = jnp.where(c_i == ((r_i >> 4) & 1) * 128 + feature, 1.0, 0.0).astype(BF16)

    def gain_of(q):
        g = gains[pl.ds(2 * q + core, 1), :]
        return jnp.where(iota((128, 128), 0) == iota((128, 128), 1), g, 0.0).astype(BF16)

    load_wq.wait()

    @pl.loop(0, NZ)
    def _(zz):
        for yy in range(NY):
            weights[zz, yy, :, 0:128] = dot(gain_of(zz * NY + yy), wq_own[zz, yy, core]).astype(BF16)

    @pl.when(sec == 0)
    def _():
        pl.semaphore_wait(barrier, 19)

    @pl.when((sec > 0) & (sec < depth - 1))
    def _():
        pl.semaphore_wait(barrier, 22)

    @pl.when(sec == depth - 1)
    def _():
        pl.semaphore_wait(barrier, 14)

    for dz in (1, 7, 2, 6, 3, 5, 4):
        slot = (dz + 1) % NZ
        send(act, rows.at[core, y, slot], s_act.at[0], r_act1.at[slot // 4], at_z(dz))
    pltpu.make_async_copy(act, rows.at[core, y, 1], r_act1.at[0]).start()

    def deal_rows():
        for dz in Z_ORDER:
            send(kvtx.at[(z + dz) % NZ], kvrx.at[z], s_kv, r_kv, at_z(dz))
        pltpu.make_async_copy(kvtx.at[z], kvrx.at[z], r_kv).start()


    @pl.when(sec == 0)
    def _():
        deal_rows()

    send(wq_own.at[:, :, 1 - core], wq_sib, s_wq, r_wq, sibling)

    for k in range(2):
        drain(rows.at[core, 0, pl.ds(0, 4)], r_act1.at[k])
        block = rows.at[core, y, pl.ds(4 * k, 4)]
        for dy in (2, 1, 3):
            send(block, block, s_act.at[1], r_act2, at_y(dy))

    @pl.when(sec > 0)
    def _():
        deal_rows()

    drain(wq_sib, r_wq)

    @pl.loop(0, NZ)
    def _(zz):
        for yy in range(NY):
            weights[zz, yy, :, 128:256] = dot(gain_of(zz * NY + yy), wq_sib[zz, yy]).astype(BF16)

    drain(rows.at[core, pl.ds(0, 3)], r_act2)
    send(rows.at[core], rows.at[core], s_act.at[2], r_act3, sibling)
    drain(rows.at[core], r_act3)

    for p in range(2):
        for yy in range(NY):
            for zz in range(NZ):
                at = ((p * NY + yy) * NZ + zz) * 40
                rowsf[at : at + 40, :] = rows[p, yy, zz].astype(F32)
    load_mw.wait()
    acc = jnp.broadcast_to(bias_ref[...].astype(F32), (64, 128))
    for k in range(20):
        xk = jnp.concatenate(
            [rowsf[pl.ds(2 * k, 64, stride=40), :], rowsf[pl.ds(2 * k + 1, 64, stride=40), :]], axis=1
        ).astype(BF16)
        acc = acc + dot(xk, mw_here[256 * k : 256 * (k + 1), :])
    part[...] = acc.astype(BF16)

    @pl.when(sec == 1)
    def _():
        send(part, merged.at[1], s_part, r_part.at[0], (0, seq, core))

    @pl.when(sec > 1)
    def _():
        send(part, merged.at[sec], s_part, r_part.at[1], (0, seq, core))

    def place(rows_here, first):
        pos = first + iota((rows_here, 1), 0)
        begin = jnp.zeros((rows_here, 1), jnp.int32)
        count = jnp.zeros((rows_here, 1), jnp.int32)
        earlier = jnp.zeros((rows_here, 1), jnp.int32)
        at, seen = jnp.int32(0), jnp.int32(0)
        for b in range(images_ref.shape[0]):
            for r in range(images_ref.shape[1]):
                image, text = images_ref[b, r], texts_ref[b, r]
                inside = pos >= at
                begin = jnp.where(inside, at, begin)
                count = jnp.where(inside, image, count)
                earlier = jnp.where(inside, seen, earlier)
                at, seen = at + image + text, seen + image
        return pos, begin, count, earlier

    def begin_batch(m):
        first, count_here = m * batch, batch
        pos, begin, count, earlier = place(count_here, first)
        offset = pos - begin
        is_image = (offset >= 1) & (offset <= count)
        row = earlier + offset - 1 - m * 128
        away = (z + NZ + 1 - ((row & 63) >> 3)) & (NZ - 1)
        slot = (row & 64) + ((row & 1) << 5) + (((row >> 1) & 3) << 3) + away
        chosen = (iota((count_here, 128), 1) == slot) & is_image
        picked = dot(
            jnp.where(chosen, 1.0, 0.0).astype(BF16), merged[2 * m : 2 * m + 2].reshape(128, 128)
        )
        text = text_ref[first : first + batch, :].astype(F32)
        start[first : first + batch, :] = jnp.where(is_image, picked, text).astype(BF16)

    def slot_of(dz):
        return (dz + 1) % NZ

    def begin_chunk(t):
        src = start.at[pl.ds(t * tc, tc)]
        for dz in SENDS:
            if dz:
                send(src, states.at[t, y, slot_of(dz)], s_init.at[t], r_st.at[t, slot_of(dz) // PER_KIND], at_z(dz))
        pltpu.make_async_copy(src, states.at[t, y, slot_of(0)], r_st.at[t, slot_of(0) // PER_KIND]).start()

    def forward(t, i):
        k = VISIT[i]
        drain(states.at[t, 0, pl.ds(0, PER_KIND)], r_st.at[t, k])
        block = states.at[t, y, pl.ds(k * PER_KIND, PER_KIND)]
        send(block, block, s_fw.at[t], r_near.at[t, k, 0], at_y(1))
        send(block, block, s_fw.at[t], r_near.at[t, k, 1], at_y(3))

    def pass_on(t, i):
        k, half = VISIT[i], PER_KIND // 2
        drain(states.at[t, 0, pl.ds(0, PER_KIND)], r_near.at[t, k, 0])
        below = states.at[t, (y + 3) % NY, pl.ds(k * PER_KIND, half)]
        send(below, below, s_fw.at[t], r_far.at[t], at_y(1))
        drain(states.at[t, 0, pl.ds(0, PER_KIND)], r_near.at[t, k, 1])
        above = states.at[t, (y + 1) % NY, pl.ds(k * PER_KIND + half, half)]
        send(above, above, s_fw.at[t], r_far.at[t], at_y(3))

    def forward_all(t):
        for k in range(KINDS):
            forward(t, k)

    def pass_on_all(t):
        for k in range(KINDS):
            pass_on(t, k)

    def forward_part(t, part_of):
        for k in range(part_of * KINDS // 2, (part_of + 1) * KINDS // 2):
            forward(t, k)

    def pass_on_part(t, part_of):
        for k in range(part_of * KINDS // 2, (part_of + 1) * KINDS // 2):
            pass_on(t, k)

    def spread_y(t):
        for k in range(KINDS):
            forward(t, k)
            if k >= 2:
                pass_on(t, k - 2)
        for k in range(max(0, KINDS - 2), KINDS):
            pass_on(t, k)

    @pl.when(sec == 0)
    def _():
        merged[0] = part[...]
        drain(merged.at[1], r_part.at[0])
        begin_batch(0)
        begin_chunk(0)
        drain(merged.at[pl.ds(2, 2)], r_part.at[1])
        begin_batch(1)

    drain(kvrx, r_kv)
    r_i, c_i = iota((128, 128), 0), iota((128, 128), 1)
    collect = ((r_i >> 5) == ((c_i >> 2) & 3)) & (((r_i >> 3) & 3) == (c_i & 3)) & ((r_i & 7) == (c_i >> 4))
    collect = jnp.where(collect, 1.0, 0.0).astype(BF16)
    for t in range(16):
        made = dot(collect, kvrx[:, t].reshape(128, 128)).astype(BF16).reshape(2, 2, 32, 128)
        for h in range(2):
            kvrows[t // 2, (t % 2) * 2 + h] = made[h]

    @pl.when(sec == 0)
    def _():
        send(kvrows.at[:, :, 1 - core], kvall.at[:, :, core], s_kvm, r_kvm, sibling)
        pltpu.make_async_copy(kvrows.at[:, :, core], kvall.at[:, :, core], r_kvm).start()
        forward_part(0, 0)
        begin_chunk(1)
        forward_part(0, 1)
        drain(kvall.at[:, :, pl.ds(0, 2)], r_kvm)

        @pl.loop(0, NZ)
        def _(zz):
            for yy in range(NY):
                mine = kvall[zz, yy, 0:2].reshape(64, 128)
                made = dot_t(gain_of(zz * NY + yy), mine)
                made = jnp.concatenate([made, jnp.zeros((128, 192), F32)], axis=1)
                weights[zz, yy, :, 256:512] = made.astype(BF16)

    @pl.when(sec > 0)
    def _():
        slot = 2 * y + core
        for i, dy in enumerate((1, 3)):
            for other in (core, 1 - core):
                to = (sec, z * NY + (y + dy) % NY, other)
                send(kvrows.at[:, :, other], kvall.at[:, :, slot], s_kvm, r_kvn.at[i], to)
        send(kvrows.at[:, :, 1 - core], kvall.at[:, :, slot], s_kvm, r_kvm, sibling)
        pltpu.make_async_copy(kvrows.at[:, :, core], kvall.at[:, :, slot], r_kvm).start()
        drain(kvall.at[:, :, pl.ds(0, 2)], r_kvn.at[0])
        below = kvall.at[:, :, 2 * ((y + 3) % NY) + 1]
        send(below, below, s_kvm, r_kvf, at_y(1))
        drain(kvall.at[:, :, pl.ds(0, 2)], r_kvn.at[1])
        above = kvall.at[:, :, 2 * ((y + 1) % NY)]
        send(above, above, s_kvm, r_kvf, at_y(3))
        drain(kvall.at[:, :, pl.ds(0, 2)], r_kvm)
        drain(kvall.at[:, :, pl.ds(0, 2)], r_kvf)

        def prepare(low, high):
            @pl.loop(low, high)
            def _(zz):
                for yy in range(NY):
                    made = dot_t(gain_of(zz * NY + yy), kvall[zz, yy].reshape(256, 128)).astype(BF16)
                    weights[zz, yy, :, 256:512] = dot(made, order[...]).astype(BF16)

        prepare(0, NZ // 2)

        @pl.when(sec == 1)
        def _():
            forward_part(0, 0)

        prepare(NZ // 2, NZ)

        @pl.when(sec == 1)
        def _():
            forward_part(0, 1)
            pass_on_all(0)

        @pl.when(sec > 1)
        def _():
            spread_y(0)

    def project(t, meanwhile=lambda: None):
        def products(ya, yb):
            def step(slot, carry):
                acc, squares = carry
                zz = (z + 2 * NZ + 1 - slot) % NZ
                x = jnp.concatenate([states[t, ya, slot], states[t, yb, slot]], axis=1)
                w = jnp.concatenate([weights[zz, ya], weights[zz, yb]], axis=0)
                acc = acc + dot(x, w)
                xf = x.astype(F32)
                for piece in (xf[:, 0:128], xf[:, 128:256]):
                    squares = squares + piece * piece
                return acc, squares

            return step

        sums = jnp.zeros((tc, 512), F32), jnp.zeros((tc, 128), F32)
        sums = lax.fori_loop(0, NZ, products(y, (y + 1) % NY), sums, unroll=8)
        drain(states.at[t, 0], r_far.at[t])
        acc, squares = lax.fori_loop(0, NZ, products((y + 2) % NY, (y + 3) % NY), sums, unroll=8)
        total = jnp.broadcast_to(jnp.sum(squares, axis=1, keepdims=True), (tc, 128))
        own_q, own_kv = acc[:, 0:128], acc[:, 256:512]
        xs[t, :, 0:128] = acc[:, 128:256]
        xs[t, :, 128:384] = own_kv
        xs[t, :, 384:512] = total
        send(xs.at[t], xr.at[t], s_x.at[t], r_x.at[t], sibling)
        meanwhile()
        drain(xr.at[t], r_x.at[t])
        scale = lax.rsqrt((total + xr[t, :, 384:512]) * (1.0 / 8192.0) + 1e-6)
        scales = jnp.concatenate([scale, scale], axis=1)
        kv = ((own_kv + xr[t, :, 128:384]) * scales).astype(BF16)
        queries[t] = ((own_q + xr[t, :, 0:128]) * scale).astype(BF16)
        return kv

    def attend(t):
        here = slice(t * tc, (t + 1) * tc)
        first = (t * tc // batch) * batch
        span = (t + 1) * tc - first
        pos, begin, _, _ = place(tc, t * tc)
        column = first + iota((tc, span), 1)
        allowed = (column >= begin) & (column <= pos)
        scores = dot_t(queries[t], keys[first : first + span, :]) * (1.0 / math.sqrt(HD))
        scores = jnp.where(allowed, scores, -1e30)
        weight = jnp.exp(scores - jnp.max(scores, axis=1, keepdims=True))
        probs = (weight / jnp.sum(weight, axis=1, keepdims=True)).astype(BF16)
        attended = dot(probs, values[first : first + span, :])
        state = states[t, y, slot_of(0)].astype(F32) + attended
        out_ref[here, :] = state.astype(BF16)

        @pl.when(sec < depth - 1)
        def _():
            for dz in SENDS:
                send(
                    out_ref.at[pl.ds(t * tc, tc)],
                    states.at[t, y, slot_of(dz)],
                    s_st.at[t],
                    r_st.at[t, slot_of(dz) // PER_KIND],
                    at_z(dz, sec + 1),
                )

    def attend_shared(t):
        here = slice(t * tc, (t + 1) * tc)
        drain(kvx.at[t, pl.ds(0, 3)], r_kx.at[t])
        kv = dot(jnp.concatenate([kvx[t, yy] for yy in range(NY)], axis=1), spread[...]).astype(BF16)
        keys[here, :] = kv[:, 0:128]
        values[here, :] = kv[:, 128:256]
        attend(t)

    @pl.when(sec == 0)
    def _():
        def first_half(t):
            if t < CHUNKS:
                forward_part(t, 0)
            if t + 1 < CHUNKS:
                begin_chunk(t + 1)

        def second_half(t):
            if t < CHUNKS:
                forward_part(t, 1)

        pass_on_all(0)
        first_half(1)
        second_half(1)
        for t in range(CHUNKS):
            kv = project(t)
            kvx[t, y] = kv[:, 0:128]
            for dy in (2, 1, 3):
                send(kvx.at[t, y], kvx.at[t, y], s_kx.at[t], r_kx.at[t], at_y(dy))
            if t + 1 < CHUNKS:
                pass_on_all(t + 1)
            first_half(t + 2)
            attend_shared(t)
            second_half(t + 2)

    @pl.when(sec > 0)
    def _():
        for t in range(CHUNKS):
            here = slice(t * tc, (t + 1) * tc)
            if t > 0:
                pass_on_part(t, 1)
            if t + 1 < CHUNKS:
                forward_all(t + 1)

            def early():
                if t + 1 < CHUNKS:
                    pass_on_part(t + 1, 0)

            kv = project(t, early)
            keys[here, :] = kv[:, 0:128]
            values[here, :] = kv[:, 128:256]
            attend(t)

    drain(rows.at[core, 0, pl.ds(0, 7)], s_act.at[0])
    drain(rows.at[core, pl.ds(0, 3)], s_act.at[1])
    drain(rows.at[core], s_act.at[2])
    drain(wq_sib, s_wq)
    drain(kvrx.at[pl.ds(0, 7)], s_kv)

    @pl.when(sec == 0)
    def _():
        drain(kvall.at[:, :, 0], s_kvm)

    @pl.when(sec > 0)
    def _():
        drain(part, s_part)
        drain(kvall.at[:, :, pl.ds(0, 7)], s_kvm)

    for t in range(CHUNKS):

        @pl.when(sec == 0)
        def _():
            drain(states.at[t, 0, pl.ds(0, 7)], s_init.at[t])
            drain(kvx.at[t, pl.ds(0, 3)], s_kx.at[t])

        @pl.when(sec < depth - 1)
        def _():
            drain(states.at[t, 0], s_st.at[t])

        drain(states.at[t, pl.ds(0, 3)], s_fw.at[t])
        drain(xs.at[t], s_x.at[t])


def shards(text_embed, patch, mw, bias, gain, wq, wk, wv, images, texts):
    tokens = text_embed.shape[0]
    tc = tokens // CHUNKS
    vmem = pl.BlockSpec(memory_space=pltpu.VMEM)
    smem = pl.BlockSpec(memory_space=pltpu.SMEM)
    hbm = pl.BlockSpec(memory_space=pl.ANY)
    dma = pltpu.SemaphoreType.DMA
    scratch = [
        pltpu.VMEM((64, 128), F32),
        pltpu.VMEM((40, 128), F32),
        pltpu.VMEM((40, 128), BF16),
        pltpu.VMEM((2, NY, NZ, 40, 128), BF16),
        pltpu.VMEM((2560, 128), F32),
        pltpu.VMEM((64, 128), BF16),
        pltpu.VMEM((4, 64, 128), BF16),
        pltpu.VMEM((tokens, 128), BF16),
        pltpu.VMEM((NZ, 16, 16, 128), BF16),
        pltpu.VMEM((NZ, 16, 16, 128), BF16),
        pltpu.VMEM((NZ, NY, 2, 32, 128), BF16),
        pltpu.VMEM((NZ, NY, 8, 32, 128), BF16),
        pltpu.VMEM((NZ, NY, 2, 128, 128), BF16),
        pltpu.VMEM((NZ, NY, 128, 128), BF16),
        pltpu.VMEM(mw.shape, BF16),
        pltpu.VMEM((NZ, NY, 128, 512), BF16),
        pltpu.VMEM((CHUNKS, NY, NZ, tc, 128), BF16),
        pltpu.VMEM((CHUNKS, tc, 512), F32),
        pltpu.VMEM((CHUNKS, tc, 512), F32),
        pltpu.VMEM((CHUNKS, NY, tc, 128), BF16),
        pltpu.VMEM((512, 256), BF16),
        pltpu.VMEM((256, 256), BF16),
        pltpu.VMEM((CHUNKS, tc, 128), BF16),
        pltpu.VMEM((tokens, 128), BF16),
        pltpu.VMEM((tokens, 128), BF16),
        dma,
        dma,
        dma((3,)),
        dma((2,)),
        dma,
        dma,
        dma,
        dma,
        dma,
        dma,
        dma,
        dma,
        dma((2,)),
        dma,
        dma,
        dma((2,)),
        dma((CHUNKS,)),
        dma((CHUNKS,)),
        dma((CHUNKS, KINDS)),
        dma((CHUNKS,)),
        dma((CHUNKS, KINDS, 2)),
        dma((CHUNKS,)),
        dma((CHUNKS,)),
        dma((CHUNKS,)),
        dma((CHUNKS,)),
        dma((CHUNKS,)),
    ]
    out = pl.pallas_call(
        kernel,
        out_shape=jax.ShapeDtypeStruct((tokens, 128), BF16),
        in_specs=[smem, smem, vmem, vmem, hbm, vmem, vmem, hbm, vmem, vmem],
        out_specs=vmem,
        scratch_shapes=scratch,
        compiler_params=pltpu.CompilerParams(
            collective_id=0, has_side_effects=True, vmem_limit_bytes=60 * 1024 * 1024
        ),
        name="prefill",
    )(
        images,
        texts,
        text_embed,
        patch,
        mw,
        bias.reshape(1, 128),
        gain,
        wq.reshape(NZ, NY, 2, 128, 128),
        jnp.swapaxes(wk[0], 0, 1),
        jnp.swapaxes(wv[0], 0, 1),
    )
    return out[None]


def solution(mesh):
    in_specs = (
        P(None, ("seq", "mp")),
        P(("section", "seq", "mp"), None),
        P(None, ("seq", "mp")),
        P(("seq", "mp")),
        P("section", None),
        P("section", None, ("seq", "mp")),
        P("section", None, ("seq", "mp")),
        P("section", None, ("seq", "mp")),
        P(),
        P(),
    )
    out_specs = P("section", None, ("seq", "mp"))
    return jax.shard_map(shards, mesh=mesh, in_specs=in_specs, out_specs=out_specs, check_vma=False)
```
